32 devices in a mesh: leaf: 8 (over z, y), blk: 4 (over x, core).
Axes of the slice: x: 2, y: 2, z: 4, core: 2. Of those that a mesh axis runs over, the one named last changes fastest.
Arguments:
- leaf_net: bfloat16 [8, 64, 4096], P('leaf'), may hold values from -1.5 to 1.5
- leaf_coupling: bfloat16 [8, 4096, 4096], P('leaf', 'blk'), as said below
- index_maps: int32 [12, 32], replicated, may hold values from 0 to 35, as said below
- sep_anchor: float32 [6, 512], replicated, may hold values from 0.5 to 4
- top_net: bfloat16 [64, 32768], P(None, 'leaf'), may hold values from -1.5 to 1.5
- top_coupling: bfloat16 [32768, 2048], P('leaf', 'blk'), as said below
Outputs:
- root_update: float32 [8, 4096, 4096], P('leaf', 'blk')
- top_window: float32 [32768, 2048], P('leaf', 'blk')
The draws below stay inside these ranges and needn't reach their ends.
Inputs may be any that keep to these rules, and one draw needn't show every extreme that they name: `index_maps`: entry i of a row sends the child's block i to block entry of the parent front: values under 512 // 128 are separator blocks, value 512 // 128 + m is block m of the parent's update matrix. Each row is one-to-one and covers every separator block. A block i that goes to the update goes to a block m with m // 2 == i // 2. Each leaf_coupling[l] is symmetric, and leaf_net[l]^T leaf_net[l] + leaf_coupling[l] is positive definite. Rows 0 to 2047 of top_coupling form a symmetric matrix, and those rows of top_net^T top_net[:, :2048] + top_coupling form a positive definite matrix.
All inputs are finite; a program needn't handle non-finite values.
Results may differ from the reference program's by a relative error of at most 0.00035.
The reference program's roundings to bfloat16 on the way count: a program that leaves them out, or rounds other values in their place, can miss the bound.
Values may be sent and summed in bfloat16 or wider, within the bound.
A program may use at most 320 MiB of HBM per device.

```python
import math
import jax
import jax.numpy as jnp
from jax import lax

BS = 128
UPD = 4096
SEP = 512
RES = 16
NETS = 64
LEVELS = 2
TOP = 32768
PW = 512
NF = 2
NODES = 12
PARENTS = 6
N_LEAF = 8
N_BLK = 4


def draw_index_maps(key, part):
    upd_blocks = UPD // BS
    sep_blocks = SEP // BS
    group_size = upd_blocks // RES
    block_ids = jnp.arange(upd_blocks, dtype=jnp.int32)
    group_of = block_ids // group_size
    place_in = block_ids % group_size

    def one_node(node_num):
        node_key = jax.random.fold_in(key, node_num)
        key_groups, key_slots, key_pick = jax.random.split(node_key, 3)
        sep_groups = jax.random.permutation(key_groups, RES - 1)[:sep_blocks].astype(jnp.int32)
        slots = jax.vmap(lambda slot_key: jax.random.permutation(slot_key, group_size))(jax.random.split(key_slots, RES)).astype(jnp.int32)
        picked = jax.random.randint(key_pick, (RES,), 0, group_size).astype(jnp.int32)
        matches = sep_groups[None, :] == jnp.arange(RES, dtype=jnp.int32)[:, None]
        sep_slot = jnp.sum(jnp.where(matches, jnp.arange(sep_blocks, dtype=jnp.int32)[None, :], 0), axis=1)
        has_sep = jnp.any(matches, axis=1)
        to_update = sep_blocks + group_of * group_size + slots[group_of, place_in]
        to_sep = has_sep[group_of] & (place_in == picked[group_of])
        return jnp.where(to_sep, sep_slot[group_of], to_update).astype(jnp.int32)
    return jax.vmap(one_node)(jnp.arange(NODES, dtype=jnp.int32))


def symmetric_block(key, order):
    key_off, key_diag = jax.random.split(key, 2)
    limit_value = 1.7 / math.sqrt(order)
    raw_draw = jax.random.uniform(key_off, (order, order), jnp.float32, -limit_value, limit_value)
    cell_ids = jnp.arange(order, dtype=jnp.int32)
    off_part = jnp.where(cell_ids[:, None] < cell_ids[None, :], raw_draw, raw_draw.T)
    diagonal = jnp.exp(jax.random.uniform(key_diag, (order,), jnp.float32, math.log(4.0), math.log(16.0)))
    return jnp.where(cell_ids[:, None] == cell_ids[None, :], diagonal[:, None], off_part)


def draw_leaf_coupling(key, part):
    leaf_keys = jax.random.split(key, N_LEAF)
    return lax.map(lambda leaf_key: symmetric_block(leaf_key, UPD).astype(jnp.bfloat16), leaf_keys)


def draw_top_coupling(key, part):
    key_block, key_below = jax.random.split(key, 2)
    win_cols = PW * N_BLK
    leading = symmetric_block(key_block, win_cols)
    below = jax.random.uniform(key_below, (TOP - win_cols, win_cols), jnp.float32, -0.5, 0.5)
    return jnp.concatenate([leading, below], axis=0).astype(jnp.bfloat16)


def levels(rng, extent, cuts, low, largest):
    loudness, own = 1.0, jax.random.fold_in(rng, 6)
    for dim, shards_of in cuts:
        steps = jnp.exp(jax.random.uniform(jax.random.fold_in(own, dim), (shards_of,), jnp.float32, low / len(cuts), largest / len(cuts)))
        loudness = loudness * jnp.repeat(steps, extent[dim] // shards_of).reshape([-1 if axis == dim else 1 for axis in range(len(extent))])
    return loudness


def bell_draw(own_key, extent, spread, bound, cuts=(), held_as=jnp.bfloat16):
    level = levels(own_key, extent, cuts, -0.22, 0.18) if cuts else 1.0
    values = jax.random.normal(own_key, extent, jnp.float32) * spread * level
    return jnp.minimum(jnp.maximum(values, -bound), bound).astype(held_as)


def setup_inputs(seed: int = 0) -> dict:
    key_of = jax.random.split(jax.random.key(seed), 7)
    leaf_net = bell_draw(key_of[0], (N_LEAF, NETS, UPD), (NETS // 4) ** -0.5, 1.5, ((0, 8),))
    leaf_coupling = draw_leaf_coupling(jax.random.fold_in(key_of[6], 71), 0)
    index_maps = draw_index_maps(jax.random.fold_in(key_of[6], 71), 0)
    sep_anchor = jnp.clip(jnp.exp(jax.random.uniform(key_of[3], (PARENTS, SEP), jnp.float32, math.log(0.5), math.log(4.0))), 0.5, 4.0)
    top_net = bell_draw(key_of[4], (NETS, TOP), (NETS // 4) ** -0.5, 1.5, ((1, 8),))
    top_coupling = draw_top_coupling(jax.random.fold_in(key_of[6], 71), 0)
    return dict(leaf_net=leaf_net, leaf_coupling=leaf_coupling, index_maps=index_maps, sep_anchor=sep_anchor, top_net=top_net, top_coupling=top_coupling)


def leaf_update(net_cols, coupling):
    gram_rows = jnp.dot(net_cols.T.astype(jnp.float32), net_cols.astype(jnp.float32), preferred_element_type=jnp.float32)
    return gram_rows + coupling.astype(jnp.float32)

def extend_add(front, update, block_map):
    positions = (block_map[:, None] * BS + jnp.arange(BS, dtype=jnp.int32)[None, :]).reshape(-1)
    return front.at[positions[:, None], positions[None, :]].add(update.astype(jnp.float32))

def eliminate(left_child, right_child, map_left, map_right, anchor_row):
    front_order = SEP + UPD
    front = jnp.zeros((front_order, front_order), jnp.float32)
    front = extend_add(front, left_child, map_left)
    front = extend_add(front, right_child, map_right)
    pivot_block = front[:SEP, :SEP] + jnp.diag(anchor_row)
    factor = jnp.linalg.cholesky(pivot_block)
    below_rows = jax.scipy.linalg.solve_triangular(factor, front[SEP:, :SEP].T, lower=True).T
    below_rows = below_rows.astype(jnp.bfloat16)
    schur_part = front[SEP:, SEP:] - jnp.dot(below_rows.astype(jnp.float32), below_rows.T.astype(jnp.float32), preferred_element_type=jnp.float32)
    return schur_part

def reference(leaf_net, leaf_coupling, index_maps, sep_anchor, top_net, top_coupling):
    updates = [leaf_update(leaf_net[leaf_num], leaf_coupling[leaf_num]) for leaf_num in range(N_LEAF)]
    node_base = 0
    parent_base = 0
    for level_num in range(LEVELS):
        parent_count = len(updates) // 2
        merged = []
        for parent_num in range(parent_count):
            merged.append(eliminate(updates[2 * parent_num], updates[2 * parent_num + 1], index_maps[node_base + 2 * parent_num], index_maps[node_base + 2 * parent_num + 1], sep_anchor[parent_base + parent_num]))
        node_base = node_base + len(updates)
        parent_base = parent_base + parent_count
        updates = merged
    root_list = jnp.stack(updates)
    root_update = jnp.repeat(root_list, 2 ** LEVELS, axis=0)
    win_cols = PW * N_BLK
    window = jnp.dot(top_net.T.astype(jnp.float32), top_net[:, :win_cols].astype(jnp.float32), preferred_element_type=jnp.float32)
    window = window + top_coupling.astype(jnp.float32)
    for panel_num in range(NF):
        panel_lo = panel_num * PW
        panel_hi = panel_lo + PW
        factor = jnp.linalg.cholesky(window[panel_lo:panel_hi, panel_lo:panel_hi])
        below_rows = jax.scipy.linalg.solve_triangular(factor, window[panel_hi:, panel_lo:panel_hi].T, lower=True).T
        panel_full = jnp.concatenate([jnp.zeros((panel_lo, PW), jnp.float32), factor, below_rows], axis=0)
        rounded = panel_full.astype(jnp.bfloat16)
        trailing = window[:, panel_hi:] - jnp.dot(rounded.astype(jnp.float32), rounded[panel_hi:win_cols].T.astype(jnp.float32), preferred_element_type=jnp.float32)
        window = jnp.concatenate([window[:, :panel_lo], panel_full, trailing], axis=1)
    return (root_update, window)
```

```python
import jax
import jax.numpy as jnp
from jax import lax
from jax.experimental import pallas as pl
from jax.experimental.pallas import tpu as pltpu
from jax.sharding import PartitionSpec as P

BS = 128
SUB = 8
PW = 512
TILE = 512
PIECE = 256
LAST = (((1,), (1,)), ((), ()))
FIRST = (((0,), (0,)), ((), ()))
HIGH = lax.Precision.HIGHEST


def gram(left, right):
    return lax.dot_general(left, right, FIRST, preferred_element_type=jnp.float32)


def outer(left, right):
    return lax.dot_general(left, right, LAST, preferred_element_type=jnp.float32)


def solved(rows, low_inverse):
    return lax.dot_general(
        rows, low_inverse, LAST, precision=HIGH, preferred_element_type=jnp.float32
    )


def exact(left, right):
    return jnp.dot(left, right, precision=HIGH, preferred_element_type=jnp.float32)


def swapped(value, axis, mask):
    return lax.ppermute(value, axis, [(s, s ^ mask) for s in range(lax.axis_size(axis))])


def total(value, axis):
    mask = 1
    while mask < lax.axis_size(axis):
        value = value + swapped(value, axis, mask)
        mask *= 2
    return value


def eliminate_block(block):
    count = BS // SUB
    full = (SUB, BS)
    row_id = lax.broadcasted_iota(jnp.int32, full, 0)
    lane_id = lax.broadcasted_iota(jnp.int32, full, 1)
    t = [block[i * SUB : (i + 1) * SUB, :] for i in range(count)]
    w = [jnp.where(lane_id == row_id + i * SUB, 1.0, 0.0) for i in range(count)]

    def lanes(i, g):
        return [
            jnp.broadcast_to(t[i][:, g * SUB + j : g * SUB + j + 1], full) for j in range(SUB)
        ]

    for g in range(count):
        c = lanes(g, g)
        tg, wg = t[g], w[g]
        row_t, row_w, scale, cross = [], [], [], []
        for j in range(SUB):
            inv = lax.rsqrt(jnp.broadcast_to(c[j][j : j + 1, :], full))
            scale.append(inv)
            row_t.append(jnp.broadcast_to(tg[j : j + 1, :], full) * inv)
            row_w.append(jnp.broadcast_to(wg[j : j + 1, :], full) * inv)
            m = c[j] * inv
            below = {}
            for q in range(j + 1, SUB):
                below[q] = jnp.broadcast_to(m[q : q + 1, :], full)
                c[q] = c[q] - m * below[q]
            cross.append(below)
            if j + 1 < SUB:
                tg = tg - m * row_t[j]
                wg = wg - m * row_w[j]
        out = row_w[0]
        for j in range(1, SUB):
            out = jnp.where(row_id == j, row_w[j], out)
        w[g] = out
        for i in range(g + 1, count):
            c = lanes(i, g)
            for j in range(SUB):
                m = c[j] * scale[j]
                for q in range(j + 1, SUB):
                    c[q] = c[q] - m * cross[j][q]
                t[i] = t[i] - m * row_t[j]
                w[i] = w[i] - m * row_w[j]
    return jnp.concatenate(w, axis=0)


def factor_kernel(block, inverse, rest):
    order = block.shape[0]
    rest[...] = block[...]
    inverse[...] = jnp.zeros_like(inverse)
    for at in range(0, order, BS):
        end = at + BS
        here = eliminate_block(rest[at:end, at:end])
        inverse[at:end, at:end] = here
        if at:
            inverse[at:end, :at] = exact(here, inverse[at:end, :at])
        if end < order:
            panel = exact(here, rest[at:end, end:])
            down = panel.T
            rest[end:, end:] = rest[end:, end:] - exact(down, panel)
            inverse[end:, :end] = inverse[end:, :end] - exact(down, inverse[at:end, :end])


def inverse_factor(block):
    order = block.shape[0]
    return pl.pallas_call(
        factor_kernel,
        out_shape=jax.ShapeDtypeStruct((order, order), jnp.float32),
        in_specs=[pl.BlockSpec(memory_space=pltpu.VMEM)],
        out_specs=pl.BlockSpec(memory_space=pltpu.VMEM),
        scratch_shapes=[pltpu.VMEM((order, order), jnp.float32)],
        compiler_params=pltpu.CompilerParams(vmem_limit_bytes=24 * 2**20),
        cost_estimate=pl.CostEstimate(
            flops=2 * 6 * order**3, bytes_accessed=8 * order**2, transcendentals=0
        ),
    )(block)


def pick_kernel(table, nets, out):
    count, depth, _ = nets.shape
    picks = table.shape[0] // count
    for q in range(count):
        for k in range(picks):
            at = table[q * picks + k]
            start = pl.multiple_of(jnp.maximum(at, 0) * BS, BS)
            piece = nets[q, :, pl.ds(start, BS)]
            out[q * depth : (q + 1) * depth, k * BS : (k + 1) * BS] = jnp.where(
                at >= 0, piece, jnp.zeros_like(piece)
            )


def pick_columns(nets, picks):
    count, depth, _ = nets.shape
    return pl.pallas_call(
        pick_kernel,
        out_shape=jax.ShapeDtypeStruct((count * depth, picks.shape[1] * BS), nets.dtype),
        in_specs=[
            pl.BlockSpec(memory_space=pltpu.SMEM),
            pl.BlockSpec(memory_space=pltpu.VMEM),
        ],
        out_specs=pl.BlockSpec(memory_space=pltpu.VMEM),
        compiler_params=pltpu.CompilerParams(vmem_limit_bytes=24 * 2**20),
    )(picks.reshape(-1), nets)


def merge_kernel(
    table, own, oth, far, low, high, l_own, l_far, l_new, n_all,
    r_own, r_far, r_new, n_rows, out, left, right,
):
    rows, tile = out.shape
    sep = l_own.shape[1]
    step = pl.program_id(0)
    half = pl.num_programs(0) // 2
    per = (table.shape[0] - 1) // 6
    first_row = table[6 * per]

    @pl.when(step == 0)
    def _():
        left[:, :sep] = -r_own[...]
        left[:, sep : 2 * sep] = -r_far[...]
        left[:, 2 * sep : 3 * sep] = -r_new[...]
        left[:, 3 * sep :] = n_rows[...]

    def spot(kind, block):
        at = table[kind * per + block]
        return at, pl.multiple_of((jnp.maximum(at, 0) % 2) * BS, BS)

    def add(ref, kind, r, piece, c, value):
        row_at, row_off = spot(kind, first_row + r)
        col_at, col_off = spot(kind, step * (tile // BS) + piece * 2 + c)
        row_off = pl.multiple_of(row_off + (r // 2) * 2 * BS, BS)
        col_off = pl.multiple_of(col_off + piece * PIECE, BS)
        got = ref[pl.ds(row_off, BS), pl.ds(col_off, BS)].astype(jnp.float32)
        return value + jnp.where((row_at >= 0) & (col_at >= 0), got, 0.0)

    for piece in range(tile // PIECE):
        for kind, ref in ((4, l_own), (5, l_far)):
            for c in range(2):
                at, off = spot(kind, step * (tile // BS) + piece * 2 + c)
                off = pl.multiple_of(off + piece * PIECE, BS)
                got = ref[pl.ds(off, BS), :]
                right[c * BS : (c + 1) * BS, (kind - 4) * sep : (kind - 3) * sep] = jnp.where(
                    at >= 0, got, jnp.zeros_like(got)
                )
        cols = slice(piece * PIECE, (piece + 1) * PIECE)
        right[:, 2 * sep : 3 * sep] = l_new[cols, :]
        right[:, 3 * sep :] = n_all[cols, :]
        for r in range(0, rows // BS, 2):
            prod = outer(left[r * BS : (r + 2) * BS, :], right[...])
            for h in range(2):
                for c in range(2):
                    value = prod[h * BS : (h + 1) * BS, c * BS : (c + 1) * BS]
                    for kind, ref in ((0, own), (1, oth), (2, far)):
                        value = add(ref, kind, r + h, piece, c, value)
                    at = piece * PIECE + c * BS
                    out[(r + h) * BS : (r + h + 1) * BS, at : at + BS] = value

    for side, ref in ((step < half, low), (step >= half, high)):

        @pl.when(side)
        def _(ref=ref):
            for piece in range(tile // PIECE):
                for r in range(rows // BS):
                    for c in range(2):
                        at = piece * PIECE + c * BS
                        spot_rows = slice(r * BS, (r + 1) * BS)
                        out[spot_rows, at : at + BS] = add(
                            ref, 3, r, piece, c, out[spot_rows, at : at + BS]
                        )


def merge(block_first, comp, node_upd, coups, factors, n_all, rows_of, n_rows):
    own, oth, far, low, high = coups
    rows, cols = own.shape
    sep = factors[0].shape[1]
    nets = n_all.shape[1]
    steps = cols // TILE
    half = steps // 2
    table = jnp.concatenate(
        [comp.reshape(-1), node_upd.reshape(-1), jnp.int32(block_first)[None]]
    )
    depth = 3 * sep + nets
    whole = lambda width: pl.BlockSpec((rows, width), lambda i: (0, 0))
    strip = lambda width: pl.BlockSpec((TILE, width), lambda i: (i, 0))
    tile = pl.BlockSpec((rows, TILE), lambda i: (0, i))
    return pl.pallas_call(
        merge_kernel,
        grid=(steps,),
        out_shape=jax.ShapeDtypeStruct((rows, cols), jnp.float32),
        in_specs=[
            pl.BlockSpec(memory_space=pltpu.SMEM),
            tile,
            tile,
            tile,
            pl.BlockSpec((rows, TILE), lambda i: (0, jnp.minimum(i, half - 1))),
            pl.BlockSpec((rows, TILE), lambda i: (0, jnp.maximum(i - half, 0))),
            strip(sep),
            strip(sep),
            strip(sep),
            strip(nets),
            whole(sep),
            whole(sep),
            whole(sep),
            whole(nets),
        ],
        out_specs=pl.BlockSpec((rows, TILE), lambda i: (0, i)),
        scratch_shapes=[
            pltpu.VMEM((rows, depth), jnp.bfloat16),
            pltpu.VMEM((PIECE, depth), jnp.bfloat16),
        ],
        compiler_params=pltpu.CompilerParams(vmem_limit_bytes=52 * 2**20),
        cost_estimate=pl.CostEstimate(
            flops=2 * rows * cols * depth,
            bytes_accessed=12 * rows * cols + 2 * cols * depth,
            transcendentals=0,
        ),
    )(table, own, oth, far, low, high, *factors, n_all, *rows_of, n_rows)


def leaf_spread(value, source_of):
    leaf_count, blk_count = lax.axis_size("leaf"), lax.axis_size("blk")
    blk_pos = lax.axis_index("blk")
    sources = jnp.array([source_of(b) for b in range(blk_count)], jnp.int32)
    rank = lax.axis_index("leaf") ^ sources[blk_pos]
    step = leaf_count // 2
    while step:
        pairs = []
        for b in range(blk_count):
            for r in range(0, leaf_count, 2 * step):
                src = source_of(b)
                pairs.append(((r ^ src) * blk_count + b, ((r + step) ^ src) * blk_count + b))
        got = lax.ppermute(value, ("leaf", "blk"), pairs)
        value = jnp.where(rank % (2 * step) == step, got, value)
        step //= 2
    return value


def first_two(value):
    blk_count = lax.axis_size("blk")
    blk_pos = lax.axis_index("blk")
    step = 2
    while step < blk_count:
        got = lax.ppermute(value, "blk", [(s, s + step) for s in range(step)])
        value = jnp.where((blk_pos >= step) & (blk_pos < 2 * step), got, value)
        step *= 2
    mate = swapped(value, "blk", 1)
    even = blk_pos % 2 == 0
    return jnp.where(even, value, mate), jnp.where(even, mate, value)


def find(match_to, ids):
    return jnp.max(jnp.where(match_to, ids, -1), axis=-1)


def take_columns(rows, src):
    return jnp.concatenate(
        [lax.dynamic_slice_in_dim(rows, src[k] * BS, BS, 1) for k in range(src.shape[0])], axis=1
    )


def take_rows(rows, picks, keeps):
    zero = jnp.zeros((), rows.dtype)
    parts = [
        jnp.where(keeps[k], lax.dynamic_slice_in_dim(rows, picks[k] * BS, BS, 0), zero)
        for k in range(picks.shape[0])
    ]
    return jnp.concatenate(parts, axis=0)


def per_device(leaf_net, leaf_coupling, index_maps, sep_anchor, top_net, top_coupling):
    leaf_count = lax.axis_size("leaf")
    leaf_pos, blk_pos = lax.axis_index("leaf"), lax.axis_index("blk")
    net_own = leaf_net[0]
    coup_own = leaf_coupling[0]
    rows_dev, upd_order = coup_own.shape
    sep_order = sep_anchor.shape[1]
    block_rows = rows_dev // BS
    sep_blocks, upd_blocks = sep_order // BS, upd_order // BS
    block_first = blk_pos * block_rows
    node = leaf_pos >> 1

    wanted = jnp.stack(
        [leaf_pos ^ q for q in range(4)] + [leaf_count + node, leaf_count + (node ^ 1)]
    )
    at = jnp.arange(index_maps.shape[0], dtype=jnp.int32)
    mine = jnp.sum(
        jnp.where(wanted[:, None, None] == at[None, :, None], index_maps[None], 0), axis=1
    )
    targets = jnp.arange(sep_blocks + upd_blocks, dtype=jnp.int32)
    ids = jnp.arange(upd_blocks, dtype=jnp.int32)
    src = find(targets[None, :, None] == mine[:, None, :], ids[None, None, :])
    leaf_src, node_src = src[:4], src[4:]
    through = jnp.repeat(node_src, 2, axis=0)
    comp = find(through[:, :, None] == ids[None, None, :], leaf_src[:, None, sep_blocks:])
    node_sep, node_upd = node_src[:, :sep_blocks], node_src[:, sep_blocks:]

    def local(table):
        return lax.dynamic_slice_in_dim(table, sep_blocks + block_first, block_rows, -1)

    def columns_and_pivot(src_row):
        sep = src_row[:sep_blocks]
        cols = take_columns(coup_own, jnp.maximum(sep, 0))
        keep = jnp.repeat(sep >= 0, BS)[None, :]
        cols = jnp.where(keep, cols, jnp.zeros((), cols.dtype))
        rows = local(src_row)
        below = take_rows(cols, jnp.maximum(rows - block_first, 0), rows >= 0)
        here = (sep >= block_first) & (sep < block_first + block_rows)
        return below, take_rows(cols, jnp.where(here, sep - block_first, 0), here)

    net_oth = swapped(net_own, "leaf", 1)
    c1_own, s1 = columns_and_pivot(leaf_src[0])
    c2_own, s2 = columns_and_pivot(comp[0])
    c1_oth = swapped(c1_own, "leaf", 1)
    s1_own = total(s1, "blk")
    s1_oth = swapped(s1_own, "leaf", 1)
    net_two = jnp.stack([net_own, net_oth])
    net_two_b, c1_oth, s1_oth, c2_b, s2_b, coup_b, top_c = lax.optimization_barrier(
        (net_two, c1_oth, s1_oth, c2_own, s2, coup_own, top_coupling)
    )

    bulk_oth = swapped(coup_b, "leaf", 1)
    bulk_far = swapped(coup_b, "leaf", 2)
    net_far = swapped(net_two_b, "leaf", 2)
    c2_oth = swapped(c2_b, "leaf", 1)
    c2_far = swapped(jnp.stack([c2_b, c2_oth]), "leaf", 2)
    s2_own = total(s2_b, "blk")
    s2_oth = swapped(s2_own, "leaf", 1)
    s2_far = swapped(jnp.stack([s2_own, s2_oth]), "leaf", 2)

    lead = 2 * PW
    rows_top = top_net.shape[1]
    piece = lax.dynamic_slice_in_dim(top_net, (blk_pos * PW) % rows_top, PW, 1)
    net_mine = leaf_spread(piece, lambda b: (b * PW) // rows_top)
    lead_mine = leaf_spread(top_c[:lead], lambda b: 0)
    both0, both1 = first_two(jnp.concatenate([lead_mine, net_mine], axis=0))
    coup0, coup1 = first_two(top_c)

    f32 = lambda value: value.astype(jnp.float32)
    pick1 = jnp.concatenate([leaf_src[:2, :sep_blocks], local(leaf_src[:2])], axis=1)
    n1 = pick_columns(net_two, pick1)
    n1_sep, n1_rows = n1[:, :sep_order], n1[:, sep_order:]
    below = gram(n1_rows, n1_sep) + f32(c1_own) + f32(c1_oth)
    pivot = gram(n1_sep, n1_sep) + f32(s1_own) + f32(s1_oth)
    low1 = inverse_factor(pivot + jnp.diag(sep_anchor[node]))
    lrow1 = solved(below, low1).astype(jnp.bfloat16)
    l_own = lax.all_gather(lrow1, "blk", axis=0, tiled=True)
    lrow1_far = swapped(lrow1, "leaf", 2)
    ones = jnp.ones((sep_blocks,), bool)
    l_sep = take_rows(l_own, node_sep[0], ones)
    l_sep_far = swapped(l_sep, "leaf", 2)
    l_far = lax.all_gather(lrow1_far, "blk", axis=0, tiled=True)

    n2 = pick_columns(jnp.concatenate([net_two_b, net_far], axis=0), comp)
    n2_sep = n2[:, :sep_order]
    n_all = n2[:, sep_order:].T
    n_rows = lax.dynamic_slice_in_dim(n_all, blk_pos * rows_dev, rows_dev, 0)

    def shuffled(rows, table):
        picks = local(table)
        return take_rows(rows, jnp.maximum(picks - block_first, 0), picks >= 0)

    r_own, r_far = shuffled(lrow1, node_src[0]), shuffled(lrow1_far, node_src[1])
    below = jnp.dot(n_rows, n2_sep, preferred_element_type=jnp.float32)
    below = below + f32(c2_own) + f32(c2_oth) + f32(c2_far[0]) + f32(c2_far[1])
    below = below - outer(r_own, l_sep) - outer(r_far, l_sep_far)
    pivot = gram(n2_sep, n2_sep) + f32(s2_own) + f32(s2_oth) + f32(s2_far[0]) + f32(s2_far[1])
    pivot = pivot - outer(l_sep, l_sep) - outer(l_sep_far, l_sep_far)
    anchor = sep_anchor[leaf_count // 2 + (node >> 1)]
    low2 = inverse_factor(pivot + jnp.diag(anchor))
    r_new = solved(below, low2).astype(jnp.bfloat16)
    l_new = lax.all_gather(r_new, "blk", axis=0, tiled=True)

    half = upd_order // 2
    bulk_low = swapped(bulk_oth[:, :half], "leaf", 2)
    bulk_high = swapped(bulk_far[:, half:], "leaf", 1)

    row = (leaf_pos * rows_top + jnp.arange(rows_top, dtype=jnp.int32))[:, None]
    col = jnp.arange(PW, dtype=jnp.int32)[None, :]

    def panel(current, low, first):
        return jnp.where(row - first >= col, solved(current, low), 0.0)

    lead0, net0 = f32(both0[:lead]), both0[lead:]
    lead1, net1 = f32(both1[:lead]), both1[lead:]
    mine = f32(lead_mine)
    inv0 = inverse_factor(gram(net0, net0) + lead0[:PW])
    cross = solved(gram(net1, net0) + lead0[PW:], inv0).astype(jnp.bfloat16)
    inv1 = inverse_factor(gram(net1, net1) + lead1[PW:] - outer(cross, cross))
    q0 = solved((gram(net0, net_mine) + mine[:PW]).T, inv0).astype(jnp.bfloat16)
    q1 = solved((gram(net1, net_mine) + mine[PW:]).T - outer(q0, cross), inv1)
    q1 = q1.astype(jnp.bfloat16)
    p0 = panel(gram(top_net, net0) + f32(coup0), inv0, 0)
    b0 = p0.astype(jnp.bfloat16)
    x1 = gram(top_net, net1) + f32(coup1) - outer(b0, cross)
    p1 = panel(x1, inv1, PW)
    rest = gram(top_net, net_mine) + f32(top_coupling) - outer(b0, q0)
    rest = rest - outer(p1.astype(jnp.bfloat16), q1)
    window = jnp.where(blk_pos == 0, p0, jnp.where(blk_pos == 1, p1, rest))

    update = merge(
        block_first,
        comp[:, sep_blocks:],
        node_upd,
        (coup_own, bulk_oth, bulk_far, bulk_low, bulk_high),
        (l_own, l_far, l_new),
        n_all,
        (r_own, r_far, r_new),
        n_rows,
    )
    return (update[None], window)


def solution(mesh):
    return jax.shard_map(
        per_device,
        mesh=mesh,
        in_specs=(
            P("leaf", None, None),
            P("leaf", "blk", None),
            P(),
            P(),
            P(None, "leaf"),
            P("leaf", "blk"),
        ),
        out_specs=(P("leaf", "blk", None), P("leaf", "blk")),
        check_vma=False,
    )
```

```python
import jax
import jax.numpy as jnp
from jax import lax
from jax.experimental import pallas as pl
from jax.experimental.pallas import tpu as pltpu
from jax.sharding import PartitionSpec as P

BS = 128
SUB = 8
PW = 512
TILE = 512
PIECE = 256
LAST = (((1,), (1,)), ((), ()))
FIRST = (((0,), (0,)), ((), ()))
HIGH = lax.Precision.HIGHEST


def gram(left, right):
    return lax.dot_general(left, right, FIRST, preferred_element_type=jnp.float32)


def outer(left, right):
    return lax.dot_general(left, right, LAST, preferred_element_type=jnp.float32)


def solved(rows, low_inverse):
    return lax.dot_general(
        rows, low_inverse, LAST, precision=HIGH, preferred_element_type=jnp.float32
    )


def exact(left, right):
    return jnp.dot(left, right, precision=HIGH, preferred_element_type=jnp.float32)


def swapped(value, axis, mask):
    return lax.ppermute(value, axis, [(s, s ^ mask) for s in range(lax.axis_size(axis))])


def total(value, axis):
    mask = 1
    while mask < lax.axis_size(axis):
        value = value + swapped(value, axis, mask)
        mask *= 2
    return value


def eliminate_block(block):
    count = BS // SUB
    full = (SUB, BS)
    row_id = lax.broadcasted_iota(jnp.int32, full, 0)
    lane_id = lax.broadcasted_iota(jnp.int32, full, 1)
    t = [block[i * SUB : (i + 1) * SUB, :] for i in range(count)]
    w = [jnp.where(lane_id == row_id + i * SUB, 1.0, 0.0) for i in range(count)]

    def lanes(i, g):
        return [
            jnp.broadcast_to(t[i][:, g * SUB + j : g * SUB + j + 1], full) for j in range(SUB)
        ]

    for g in range(count):
        c = lanes(g, g)
        tg, wg = t[g], w[g]
        row_t, row_w, scale, cross = [], [], [], []
        for j in range(SUB):
            inv = lax.rsqrt(jnp.broadcast_to(c[j][j : j + 1, :], full))
            scale.append(inv)
            row_t.append(jnp.broadcast_to(tg[j : j + 1, :], full) * inv)
            row_w.append(jnp.broadcast_to(wg[j : j + 1, :], full) * inv)
            m = c[j] * inv
            below = {}
            for q in range(j + 1, SUB):
                below[q] = jnp.broadcast_to(m[q : q + 1, :], full)
                c[q] = c[q] - m * below[q]
            cross.append(below)
            if j + 1 < SUB:
                tg = tg - m * row_t[j]
                wg = wg - m * row_w[j]
        out = row_w[0]
        for j in range(1, SUB):
            out = jnp.where(row_id == j, row_w[j], out)
        w[g] = out
        for i in range(g + 1, count):
            c = lanes(i, g)
            for j in range(SUB):
                m = c[j] * scale[j]
                for q in range(j + 1, SUB):
                    c[q] = c[q] - m * cross[j][q]
                t[i] = t[i] - m * row_t[j]
                w[i] = w[i] - m * row_w[j]
    return jnp.concatenate(w, axis=0)


def factor_kernel(block, inverse, rest):
    order = block.shape[0]
    rest[...] = block[...]
    inverse[...] = jnp.zeros_like(inverse)
    for at in range(0, order, BS):
        end = at + BS
        here = eliminate_block(rest[at:end, at:end])
        inverse[at:end, at:end] = here
        if at:
            inverse[at:end, :at] = exact(here, inverse[at:end, :at])
        if end < order:
            panel = exact(here, rest[at:end, end:])
            down = panel.T
            rest[end:, end:] = rest[end:, end:] - exact(down, panel)
            inverse[end:, :end] = inverse[end:, :end] - exact(down, inverse[at:end, :end])


def inverse_factor(block):
    order = block.shape[0]
    return pl.pallas_call(
        factor_kernel,
        out_shape=jax.ShapeDtypeStruct((order, order), jnp.float32),
        in_specs=[pl.BlockSpec(memory_space=pltpu.VMEM)],
        out_specs=pl.BlockSpec(memory_space=pltpu.VMEM),
        scratch_shapes=[pltpu.VMEM((order, order), jnp.float32)],
        compiler_params=pltpu.CompilerParams(vmem_limit_bytes=24 * 2**20),
        cost_estimate=pl.CostEstimate(
            flops=2 * 6 * order**3, bytes_accessed=8 * order**2, transcendentals=0
        ),
    )(block)


def table_kernel(sep_blocks, maps, who, out):
    upd_blocks = maps.shape[1]
    per = sep_blocks + upd_blocks

    def clear(e, _):
        out[e] = -1
        return 0

    lax.fori_loop(0, 10 * per, clear, 0, unroll=8)
    for q in range(6):
        node = who[q]

        def place(i, _, q=q, node=node):
            out[q * per + maps[node, i]] = i
            return 0

        lax.fori_loop(0, upd_blocks, place, 0, unroll=8)
    for q in range(4):

        def chain(e, _, q=q):
            k = out[(4 + q // 2) * per + e]
            got = out[q * per + sep_blocks + jnp.maximum(k, 0)]
            out[(6 + q) * per + e] = jnp.where(k >= 0, got, -1)
            return 0

        lax.fori_loop(0, per, chain, 0, unroll=6)
    for k in range(who.shape[0] - 6):
        out[10 * per + k] = who[6 + k]


def make_table(index_maps, sep_blocks, who):
    entries = 10 * (sep_blocks + index_maps.shape[1]) + who.shape[0] - 6
    return pl.pallas_call(
        lambda maps, who, out: table_kernel(sep_blocks, maps, who, out),
        out_shape=jax.ShapeDtypeStruct((entries,), jnp.int32),
        in_specs=[pl.BlockSpec(memory_space=pltpu.SMEM)] * 2,
        out_specs=pl.BlockSpec(memory_space=pltpu.SMEM),
    )(index_maps, who)


LEAF, NODE, BOTH = 0, 4, 6


class Layout:
    def __init__(self, sep_blocks, upd_blocks):
        self.sep = sep_blocks
        self.per = sep_blocks + upd_blocks
        self.first = 10 * self.per

    def sep_at(self, table, row, s):
        return table[row * self.per + s]

    def upd_at(self, table, row, m):
        return table[row * self.per + self.sep + m]


def block_start(at):
    return pl.multiple_of(jnp.maximum(at, 0) * BS, BS)


def pair_start(at):
    return pl.multiple_of((jnp.maximum(at, 0) % 2) * BS, BS)


def kept(keep, value):
    return jnp.where(keep, value, jnp.zeros_like(value))


def extract_kernel(lay, table, coup, c1, s1, c2, s2):
    step = pl.program_id(0)
    group = table[lay.first] // 2 + step

    @pl.when(step == 0)
    def _():
        s1[...] = jnp.zeros_like(s1)
        s2[...] = jnp.zeros_like(s2)

    for row, below, pivot in ((LEAF, c1, s1), (BOTH, c2, s2)):
        for s in range(lay.sep):
            col = lay.sep_at(table, row, s)
            cols = pl.ds(block_start(col), BS)
            at = slice(s * BS, (s + 1) * BS)
            for h in range(2):
                src = lay.upd_at(table, row, 2 * group + h)
                got = coup[pl.ds(pair_start(src), BS), cols]
                below[h * BS : (h + 1) * BS, at] = kept((src >= 0) & (col >= 0), got)
            for r in range(lay.sep):
                src = lay.sep_at(table, row, r)

                @pl.when((src >= 0) & (src // 2 == group))
                def _(src=src, r=r, at=at, cols=cols, col=col, pivot=pivot):
                    got = coup[pl.ds(pair_start(src), BS), cols]
                    pivot[r * BS : (r + 1) * BS, at] = kept(col >= 0, got)


def extract(lay, table, coup):
    rows, width = coup.shape
    sep = lay.sep * BS
    below = jax.ShapeDtypeStruct((rows, sep), coup.dtype)
    pivot = jax.ShapeDtypeStruct((sep, sep), coup.dtype)
    strip = pl.BlockSpec((2 * BS, sep), lambda i: (i, 0))
    fixed = pl.BlockSpec((sep, sep), lambda i: (0, 0))
    return pl.pallas_call(
        lambda *refs: extract_kernel(lay, *refs),
        grid=(rows // (2 * BS),),
        out_shape=(below, pivot, below, pivot),
        in_specs=[
            pl.BlockSpec(memory_space=pltpu.SMEM),
            pl.BlockSpec((2 * BS, width), lambda i: (i, 0)),
        ],
        out_specs=(strip, fixed, strip, fixed),
        compiler_params=pltpu.CompilerParams(vmem_limit_bytes=24 * 2**20),
    )(table, coup)


def pick_kernel(picks, table, *refs):
    nets, out = refs[:-1], refs[-1]
    depth = nets[0].shape[0]
    for q, net in enumerate(nets):
        for k, pick in enumerate(picks):
            at = pick(table, q)
            out[q * depth : (q + 1) * depth, k * BS : (k + 1) * BS] = kept(
                at >= 0, net[:, pl.ds(block_start(at), BS)]
            )


def pick_columns(picks, table, nets):
    return pl.pallas_call(
        lambda *refs: pick_kernel(picks, *refs),
        out_shape=jax.ShapeDtypeStruct(
            (len(nets) * nets[0].shape[0], len(picks) * BS), nets[0].dtype
        ),
        in_specs=[pl.BlockSpec(memory_space=pltpu.SMEM)]
        + [pl.BlockSpec(memory_space=pltpu.VMEM)] * len(nets),
        out_specs=pl.BlockSpec(memory_space=pltpu.VMEM),
        compiler_params=pltpu.CompilerParams(vmem_limit_bytes=24 * 2**20),
    )(table, *nets)


def front_kernel(lay, table, l_row, far_row, l_sep, far_sep, n_rows, n_sep, *refs):
    coups, (below, r_own, r_far) = refs[:-3], refs[-3:]
    group = table[lay.first] // 2 + pl.program_id(0)
    for p, row, out in ((0, l_row, r_own), (1, far_row, r_far)):
        for h in range(2):
            src = lay.upd_at(table, NODE + p, 2 * group + h)
            out[h * BS : (h + 1) * BS, :] = kept(src >= 0, row[pl.ds(pair_start(src), BS), :])
    value = jnp.dot(n_rows[...], n_sep[...], preferred_element_type=jnp.float32)
    for ref in coups:
        value = value + ref[...].astype(jnp.float32)
    value = value - outer(r_own[...], l_sep[...])
    below[...] = value - outer(r_far[...], far_sep[...])


def front(lay, table, l_row, far_row, l_sep, far_sep, n_rows, n_sep, coups):
    rows, sep = l_row.shape
    nets = n_rows.shape[1]
    strip = pl.BlockSpec((2 * BS, sep), lambda i: (i, 0))
    fixed = pl.BlockSpec((sep, sep), lambda i: (0, 0))
    picked = jax.ShapeDtypeStruct((rows, sep), l_row.dtype)
    return pl.pallas_call(
        lambda *refs: front_kernel(lay, *refs),
        grid=(rows // (2 * BS),),
        out_shape=(jax.ShapeDtypeStruct((rows, sep), jnp.float32), picked, picked),
        in_specs=[
            pl.BlockSpec(memory_space=pltpu.SMEM),
            strip,
            strip,
            fixed,
            fixed,
            pl.BlockSpec((2 * BS, nets), lambda i: (i, 0)),
            pl.BlockSpec((nets, sep), lambda i: (0, 0)),
        ]
        + [strip] * len(coups),
        out_specs=(strip, strip, strip),
        compiler_params=pltpu.CompilerParams(vmem_limit_bytes=24 * 2**20),
    )(table, l_row, far_row, l_sep, far_sep, n_rows, n_sep, *coups)


def copy_kernel(table, rows, out):
    out[...] = rows[...]


def pick_rows(lay, table, row, rows):
    width = rows.shape[1]
    spec = pltpu.PrefetchScalarGridSpec(
        num_scalar_prefetch=1,
        grid=(lay.sep,),
        in_specs=[
            pl.BlockSpec((BS, width), lambda i, t: (jnp.maximum(t[row * lay.per + i], 0), 0))
        ],
        out_specs=pl.BlockSpec((BS, width), lambda i, t: (i, 0)),
    )
    return pl.pallas_call(
        copy_kernel,
        out_shape=jax.ShapeDtypeStruct((lay.sep * BS, width), rows.dtype),
        grid_spec=spec,
    )(table, rows)


def merge_kernel(
    lay, table, own, *refs
):
    bulk = refs[:15]
    (l_own, l_far, l_new, n_all, r_own, r_far, r_new, n_rows, out) = refs[15:24]
    left, right, turn, turned = refs[24:]
    rows, tile = out.shape
    sep = l_own.shape[1]
    step = pl.program_id(0)
    kind, side = step // 2, step % 2
    first_row = table[lay.first]
    col_tile = (table[lay.first + 1 + kind] * 2 + side) * (tile // BS)
    even = table[lay.first] // (rows // BS) % 2 == 0
    others = (1, 2, 3)

    @pl.when(step == 0)
    def _():
        left[:, :sep] = -r_own[...]
        left[:, sep : 2 * sep] = -r_far[...]
        left[:, 2 * sep : 3 * sep] = -r_new[...]
        left[:, 3 * sep :] = n_rows[...]
        lane = lax.broadcasted_iota(jnp.int32, (BS, 2 * BS), 1)
        row = lax.broadcasted_iota(jnp.int32, (BS, 2 * BS), 0)
        for r in range(rows // BS):
            for n, q in enumerate(others):
                at = lay.upd_at(table, BOTH + q, first_row + r)
                hit = (lane == row + pair_start(at)) & (at >= 0)
                turn[r * BS : (r + 1) * BS, n * PIECE : (n + 1) * PIECE] = jnp.where(
                    hit, 1.0, 0.0
                ).astype(jnp.bfloat16)

    def col_of(piece, c):
        return col_tile + piece * 2 + c

    def add(ref, q, r, piece, c, value):
        row_at = lay.upd_at(table, BOTH + q, first_row + r)
        col_at = lay.upd_at(table, BOTH + q, col_of(piece, c))
        row_off = pl.multiple_of(pair_start(row_at) + (r // 2) * 2 * BS, BS)
        col_off = pl.multiple_of(pair_start(col_at) + piece * PIECE, BS)
        got = ref[pl.ds(row_off, BS), pl.ds(col_off, BS)].astype(jnp.float32)
        return value + jnp.where((row_at >= 0) & (col_at >= 0), got, 0.0)

    for piece in range(tile // PIECE):
        for p, ref in ((0, l_own), (1, l_far)):
            for c in range(2):
                at = lay.upd_at(table, NODE + p, col_of(piece, c))
                off = pl.multiple_of(pair_start(at) + piece * PIECE, BS)
                right[c * BS : (c + 1) * BS, p * sep : (p + 1) * sep] = kept(
                    at >= 0, ref[pl.ds(off, BS), :]
                )
        cols = slice(piece * PIECE, (piece + 1) * PIECE)
        right[:, 2 * sep : 3 * sep] = l_new[cols, :]
        right[:, 3 * sep :] = n_all[cols, :]
        for r in range(0, rows // BS, 2):
            prod = outer(left[r * BS : (r + 2) * BS, :], right[...])
            for h in range(2):
                for c in range(2):
                    value = prod[h * BS : (h + 1) * BS, c * BS : (c + 1) * BS]
                    at = piece * PIECE + c * BS
                    out[(r + h) * BS : (r + h + 1) * BS, at : at + BS] = add(
                        own, 0, r + h, piece, c, value
                    )

    def direct(sources):
        for piece in range(tile // PIECE):
            for r in range(rows // BS):
                for c in range(2):
                    spot = (
                        slice(r * BS, (r + 1) * BS),
                        slice(piece * PIECE + c * BS, piece * PIECE + (c + 1) * BS),
                    )
                    value = out[spot]
                    for q, ref in zip(others, sources):
                        value = add(ref, q, r, piece, c, value)
                    out[spot] = value

    def transposed(sources):
        width = len(others) * PIECE
        for piece in range(tile // PIECE):
            for c in range(2):
                for n, (q, ref) in enumerate(zip(others, sources)):
                    at = lay.upd_at(table, BOTH + q, col_of(piece, c))
                    off = pl.multiple_of(pair_start(at) + piece * PIECE, BS)
                    got = kept(at >= 0, ref[pl.ds(off, BS), :])
                    for g in range(rows // PIECE):
                        to = g * width + n * PIECE
                        turned[c * BS : (c + 1) * BS, to : to + PIECE] = got[
                            :, g * PIECE : (g + 1) * PIECE
                        ]
            cols = slice(piece * PIECE, (piece + 1) * PIECE)
            for g in range(rows // PIECE):
                spot = slice(g * PIECE, (g + 1) * PIECE)
                out[spot, cols] = out[spot, cols] + outer(
                    turn[spot, :], turned[:, g * width : (g + 1) * width]
                )

    for case, run, at in (
        (kind == 0, direct, 0),
        (kind == 1, direct, 3),
        (kind == 2, transposed, 6),
        ((kind == 3) & even, direct, 9),
        ((kind == 3) & jnp.logical_not(even), transposed, 12),
    ):

        @pl.when(case)
        def _(run=run, at=at):
            run(bulk[at : at + 3])


def merge(lay, table, own, diag, follow, turned, extra, extra_turned, factors, n_all, rows_of, n_rows):
    rows, cols = own.shape
    sep = factors[0].shape[1]
    nets = n_all.shape[1]
    depth = 3 * sep + nets
    strip_at = lambda i, t: t[lay.first + 1 + i // 2] * 2 + i % 2
    once = pl.Buffered(1)
    whole = lambda width: pl.BlockSpec((rows, width), lambda i, t: (0, 0), pipeline_mode=once)
    strip = lambda width: pl.BlockSpec((TILE, width), lambda i, t: (strip_at(i, t), 0))
    tile = pl.BlockSpec((rows, TILE), lambda i, t: (0, strip_at(i, t)))

    def wide(k):
        return pl.BlockSpec((rows, TILE), lambda i, t: (0, jnp.clip(i - 2 * k, 0, 1)))

    def tall(k):
        return pl.BlockSpec((TILE, rows), lambda i, t: (jnp.clip(i - 2 * k, 0, 1), 0))

    spec = pltpu.PrefetchScalarGridSpec(
        num_scalar_prefetch=1,
        grid=(cols // TILE,),
        in_specs=[tile]
        + [wide(0)] * 3
        + [wide(1)] * 3
        + [tall(2)] * 3
        + [wide(3)] * 3
        + [tall(3)] * 3
        + [strip(sep)] * 3
        + [strip(nets)]
        + [whole(sep)] * 3
        + [whole(nets)],
        out_specs=tile,
        scratch_shapes=[
            pltpu.VMEM((rows, depth), jnp.bfloat16),
            pltpu.VMEM((PIECE, depth), jnp.bfloat16),
            pltpu.VMEM((rows, 3 * PIECE), jnp.bfloat16),
            pltpu.VMEM((PIECE, 3 * rows), jnp.bfloat16),
        ],
    )
    return pl.pallas_call(
        lambda *refs: merge_kernel(lay, *refs),
        out_shape=jax.ShapeDtypeStruct((rows, cols), jnp.float32),
        grid_spec=spec,
        compiler_params=pltpu.CompilerParams(vmem_limit_bytes=56 * 2**20),
        cost_estimate=pl.CostEstimate(
            flops=2 * rows * cols * depth,
            bytes_accessed=12 * rows * cols + 2 * cols * depth,
            transcendentals=0,
        ),
    )(
        table, own, *diag, *follow, *turned, *extra, *extra_turned, *factors, n_all, *rows_of, n_rows
    )


def plain_merge_kernel(
    table, own, oth, far, low, high, l_own, l_far, l_new, n_all,
    r_own, r_far, r_new, n_rows, out, left, right,
):
    rows, tile = out.shape
    sep = l_own.shape[1]
    step = pl.program_id(0)
    half = pl.num_programs(0) // 2
    per = (table.shape[0] - 1) // 6
    first_row = table[6 * per]

    @pl.when(step == 0)
    def _():
        left[:, :sep] = -r_own[...]
        left[:, sep : 2 * sep] = -r_far[...]
        left[:, 2 * sep : 3 * sep] = -r_new[...]
        left[:, 3 * sep :] = n_rows[...]

    def spot(kind, block):
        at = table[kind * per + block]
        return at, pl.multiple_of((jnp.maximum(at, 0) % 2) * BS, BS)

    def add(ref, kind, r, piece, c, value):
        row_at, row_off = spot(kind, first_row + r)
        col_at, col_off = spot(kind, step * (tile // BS) + piece * 2 + c)
        row_off = pl.multiple_of(row_off + (r // 2) * 2 * BS, BS)
        col_off = pl.multiple_of(col_off + piece * PIECE, BS)
        got = ref[pl.ds(row_off, BS), pl.ds(col_off, BS)].astype(jnp.float32)
        return value + jnp.where((row_at >= 0) & (col_at >= 0), got, 0.0)

    for piece in range(tile // PIECE):
        for kind, ref in ((4, l_own), (5, l_far)):
            for c in range(2):
                at, off = spot(kind, step * (tile // BS) + piece * 2 + c)
                off = pl.multiple_of(off + piece * PIECE, BS)
                got = ref[pl.ds(off, BS), :]
                right[c * BS : (c + 1) * BS, (kind - 4) * sep : (kind - 3) * sep] = jnp.where(
                    at >= 0, got, jnp.zeros_like(got)
                )
        cols = slice(piece * PIECE, (piece + 1) * PIECE)
        right[:, 2 * sep : 3 * sep] = l_new[cols, :]
        right[:, 3 * sep :] = n_all[cols, :]
        for r in range(0, rows // BS, 2):
            prod = outer(left[r * BS : (r + 2) * BS, :], right[...])
            for h in range(2):
                for c in range(2):
                    value = prod[h * BS : (h + 1) * BS, c * BS : (c + 1) * BS]
                    for kind, ref in ((0, own), (1, oth), (2, far)):
                        value = add(ref, kind, r + h, piece, c, value)
                    at = piece * PIECE + c * BS
                    out[(r + h) * BS : (r + h + 1) * BS, at : at + BS] = value

    for side, ref in ((step < half, low), (step >= half, high)):

        @pl.when(side)
        def _(ref=ref):
            for piece in range(tile // PIECE):
                for r in range(rows // BS):
                    for c in range(2):
                        at = piece * PIECE + c * BS
                        spot_rows = slice(r * BS, (r + 1) * BS)
                        out[spot_rows, at : at + BS] = add(
                            ref, 3, r, piece, c, out[spot_rows, at : at + BS]
                        )


def plain_merge(block_first, comp, node_upd, coups, factors, n_all, rows_of, n_rows):
    own, oth, far, low, high = coups
    rows, cols = own.shape
    sep = factors[0].shape[1]
    nets = n_all.shape[1]
    steps = cols // TILE
    half = steps // 2
    table = jnp.concatenate(
        [comp.reshape(-1), node_upd.reshape(-1), jnp.int32(block_first)[None]]
    )
    depth = 3 * sep + nets
    whole = lambda width: pl.BlockSpec((rows, width), lambda i: (0, 0))
    strip = lambda width: pl.BlockSpec((TILE, width), lambda i: (i, 0))
    tile = pl.BlockSpec((rows, TILE), lambda i: (0, i))
    return pl.pallas_call(
        plain_merge_kernel,
        grid=(steps,),
        out_shape=jax.ShapeDtypeStruct((rows, cols), jnp.float32),
        in_specs=[
            pl.BlockSpec(memory_space=pltpu.SMEM),
            tile,
            tile,
            tile,
            pl.BlockSpec((rows, TILE), lambda i: (0, jnp.minimum(i, half - 1))),
            pl.BlockSpec((rows, TILE), lambda i: (0, jnp.maximum(i - half, 0))),
            strip(sep),
            strip(sep),
            strip(sep),
            strip(nets),
            whole(sep),
            whole(sep),
            whole(sep),
            whole(nets),
        ],
        out_specs=pl.BlockSpec((rows, TILE), lambda i: (0, i)),
        scratch_shapes=[
            pltpu.VMEM((rows, depth), jnp.bfloat16),
            pltpu.VMEM((PIECE, depth), jnp.bfloat16),
        ],
        compiler_params=pltpu.CompilerParams(vmem_limit_bytes=52 * 2**20),
        cost_estimate=pl.CostEstimate(
            flops=2 * rows * cols * depth,
            bytes_accessed=12 * rows * cols + 2 * cols * depth,
            transcendentals=0,
        ),
    )(table, own, oth, far, low, high, *factors, n_all, *rows_of, n_rows)


def leaf_spread(value, source_of):
    leaf_count, blk_count = lax.axis_size("leaf"), lax.axis_size("blk")
    blk_pos = lax.axis_index("blk")
    sources = jnp.array([source_of(b) for b in range(blk_count)], jnp.int32)
    rank = lax.axis_index("leaf") ^ sources[blk_pos]
    step = leaf_count // 2
    while step:
        pairs = []
        for b in range(blk_count):
            for r in range(0, leaf_count, 2 * step):
                src = source_of(b)
                pairs.append(((r ^ src) * blk_count + b, ((r + step) ^ src) * blk_count + b))
        got = lax.ppermute(value, ("leaf", "blk"), pairs)
        value = jnp.where(rank % (2 * step) == step, got, value)
        step //= 2
    return value


def first_two(value):
    blk_count = lax.axis_size("blk")
    blk_pos = lax.axis_index("blk")
    step = 2
    while step < blk_count:
        got = lax.ppermute(value, "blk", [(s, s + step) for s in range(step)])
        value = jnp.where((blk_pos >= step) & (blk_pos < 2 * step), got, value)
        step *= 2
    mate = swapped(value, "blk", 1)
    even = blk_pos % 2 == 0
    return jnp.where(even, value, mate), jnp.where(even, mate, value)


def per_device(leaf_net, leaf_coupling, index_maps, sep_anchor, top_net, top_coupling):
    leaf_count, blk_count = lax.axis_size("leaf"), lax.axis_size("blk")
    leaf_pos, blk_pos = lax.axis_index("leaf"), lax.axis_index("blk")
    net_own = leaf_net[0]
    coup_own = leaf_coupling[0]
    rows_dev, upd_order = coup_own.shape
    sep_order = sep_anchor.shape[1]
    block_rows = rows_dev // BS
    lay = Layout(sep_order // BS, upd_order // BS)
    block_first = blk_pos * block_rows
    node = leaf_pos >> 1
    triangle = blk_count == 4
    f32 = lambda value: value.astype(jnp.float32)
    tie = lax.optimization_barrier

    def among(options):
        return jnp.array(options, jnp.int32)[blk_pos]

    follow_to = (2, 3, 1, 0)
    places = [block_first]
    if triangle:
        places += [blk_pos, among(follow_to), among((3, 2, 0, 1)), blk_pos ^ 1]
    who = [leaf_pos ^ q for q in range(4)] + [leaf_count + node, leaf_count + (node ^ 1)]
    table = make_table(index_maps, lay.sep, jnp.stack(who + places))

    net_oth = swapped(net_own, "leaf", 1)
    c1_own, s1, c2_own, s2 = extract(lay, table, coup_own)
    c1_oth = swapped(c1_own, "leaf", 1)
    s1_own = total(s1, "blk")
    s1_oth = swapped(s1_own, "leaf", 1)

    pick1 = [lambda t, q, s=s: lay.sep_at(t, LEAF + q, s) for s in range(lay.sep)]
    pick1 += [
        lambda t, q, i=i: lay.upd_at(t, LEAF + q, t[lay.first] + i) for i in range(block_rows)
    ]
    n1 = pick_columns(pick1, table, [net_own, net_oth])
    n1_sep, n1_rows = n1[:, :sep_order], n1[:, sep_order:]
    below = gram(n1_rows, n1_sep) + f32(c1_own) + f32(c1_oth)
    pivot = gram(n1_sep, n1_sep) + f32(s1_own) + f32(s1_oth) + jnp.diag(sep_anchor[node])

    pivot, net_b, net_oth_b, c2_b, s2_b, top_c = tie(
        (pivot, net_own, net_oth, c2_own, s2, top_coupling)
    )
    net_far, net_far_oth = swapped(net_b, "leaf", 2), swapped(net_oth_b, "leaf", 2)
    c2_oth = swapped(c2_b, "leaf", 1)
    c2_far, c2_far_oth = swapped(c2_b, "leaf", 2), swapped(c2_oth, "leaf", 2)
    s2_own = total(s2_b, "blk")
    s2_oth = swapped(s2_own, "leaf", 1)
    s2_far, s2_far_oth = swapped(s2_own, "leaf", 2), swapped(s2_oth, "leaf", 2)

    lead = 2 * PW
    rows_top = top_net.shape[1]
    piece = lax.dynamic_slice_in_dim(top_net, (blk_pos * PW) % rows_top, PW, 1)
    net_mine = leaf_spread(piece, lambda b: (b * PW) // rows_top)
    lead_mine = leaf_spread(top_c[:lead], lambda b: 0)
    both0, both1 = first_two(jnp.concatenate([lead_mine, net_mine], axis=0))
    coup0, coup1 = first_two(top_c)

    low1 = inverse_factor(pivot)
    lrow1 = solved(below, low1).astype(jnp.bfloat16)
    l_own = lax.all_gather(lrow1, "blk", axis=0, tiled=True)
    lrow1_far = swapped(lrow1, "leaf", 2)
    l_sep = pick_rows(lay, table, NODE, l_own)
    l_sep_far = swapped(l_sep, "leaf", 2)
    l_far = lax.all_gather(lrow1_far, "blk", axis=0, tiled=True)

    def leaf_even(value, mask):
        pairs = [
            (l * blk_count + b, (l ^ mask) * blk_count + b)
            for l in range(leaf_count)
            for b in range(0, blk_count, 2)
        ]
        return lax.ppermute(value, ("leaf", "blk"), pairs)

    if triangle:
        coup_b, _ = tie((coup_own, c2_oth))
        block = lambda src, c: lax.dynamic_slice_in_dim(src, c * rows_dev, rows_dev, 1)
        follow0 = block(coup_b, among(follow_to))
        follow1, follow2 = swapped(follow0, "leaf", 1), swapped(follow0, "leaf", 2)
        diag0 = block(coup_b, blk_pos)
        extra0 = block(coup_b, blk_pos ^ 1)
        diag1, extra1 = swapped(diag0, "leaf", 1), leaf_even(extra0, 1)
        diag0, extra0, l_sep_far, follow1, follow2 = tie(
            (diag0, extra0, l_sep_far, follow1, follow2)
        )
        extra2, diag2 = leaf_even(extra0, 2), swapped(diag0, "leaf", 2)
        follow3 = swapped(follow1, "leaf", 2)
        turn = lambda value: lax.ppermute(
            value, "blk", [(b, follow_to[b]) for b in range(blk_count)]
        )
        to_odd = lambda value: lax.ppermute(
            value, "blk", [(b, b + 1) for b in range(0, blk_count, 2)]
        )
        turned1, turned2 = turn(follow1), turn(follow2)
        low_extra1 = to_odd(extra1)

    pick2 = [lambda t, q, s=s: lay.sep_at(t, BOTH + q, s) for s in range(lay.sep)]
    pick2 += [lambda t, q, m=m: lay.upd_at(t, BOTH + q, m) for m in range(upd_order // BS)]
    n2 = pick_columns(pick2, table, [net_own, net_oth, net_far, net_far_oth])
    n2_sep = n2[:, :sep_order]
    n_all = n2[:, sep_order:].T
    n_rows = lax.dynamic_slice_in_dim(n_all, blk_pos * rows_dev, rows_dev, 0)

    below, r_own, r_far = front(
        lay, table, lrow1, lrow1_far, l_sep, l_sep_far, n_rows, n2_sep,
        (c2_own, c2_oth, c2_far, c2_far_oth),
    )
    pivot = gram(n2_sep, n2_sep) + f32(s2_own) + f32(s2_oth) + f32(s2_far) + f32(s2_far_oth)
    pivot = pivot - outer(l_sep, l_sep) - outer(l_sep_far, l_sep_far)
    low2 = inverse_factor(pivot + jnp.diag(sep_anchor[leaf_count // 2 + (node >> 1)]))
    r_new = solved(below, low2).astype(jnp.bfloat16)
    l_new = lax.all_gather(r_new, "blk", axis=0, tiled=True)

    row = (leaf_pos * rows_top + jnp.arange(rows_top, dtype=jnp.int32))[:, None]
    col = jnp.arange(PW, dtype=jnp.int32)[None, :]

    def panel(current, low, first):
        return jnp.where(row - first >= col, solved(current, low), 0.0)

    lead0, net0 = f32(both0[:lead]), both0[lead:]
    lead1, net1 = f32(both1[:lead]), both1[lead:]
    mine = f32(lead_mine)
    inv0 = inverse_factor(gram(net0, net0) + lead0[:PW])
    cross = solved(gram(net1, net0) + lead0[PW:], inv0).astype(jnp.bfloat16)
    inv1 = inverse_factor(gram(net1, net1) + lead1[PW:] - outer(cross, cross))
    if triangle:
        inv1, diag1, extra1, diag2, extra2, follow3, r_new = tie(
            (inv1, diag1, extra1, diag2, extra2, follow3, r_new)
        )
        diag3, extra3 = swapped(diag2, "leaf", 1), leaf_even(extra2, 1)
        low_extra2, low_extra3 = to_odd(extra2), to_odd(extra3)
        turned3 = turn(follow3)
    q0 = solved((gram(net0, net_mine) + mine[:PW]).T, inv0).astype(jnp.bfloat16)
    q1 = solved((gram(net1, net_mine) + mine[PW:]).T - outer(q0, cross), inv1)
    q1 = q1.astype(jnp.bfloat16)
    p0 = panel(gram(top_net, net0) + f32(coup0), inv0, 0)
    b0 = p0.astype(jnp.bfloat16)
    x1 = gram(top_net, net1) + f32(coup1) - outer(b0, cross)
    p1 = panel(x1, inv1, PW)
    rest = gram(top_net, net_mine) + f32(top_coupling) - outer(b0, q0)
    rest = rest - outer(p1.astype(jnp.bfloat16), q1)
    window = jnp.where(blk_pos == 0, p0, jnp.where(blk_pos == 1, p1, rest))

    factors, rows_of = (l_own, l_far, l_new), (r_own, r_far, r_new)
    if triangle:
        update = merge(
            lay, table, coup_own,
            (diag1, diag2, diag3),
            (follow1, follow2, follow3),
            (turned1, turned2, turned3),
            (extra1, extra2, extra3),
            (low_extra1, low_extra2, low_extra3),
            factors, n_all, rows_of, n_rows,
        )
    else:
        half = upd_order // 2
        bulk_oth, bulk_far = swapped(coup_own, "leaf", 1), swapped(coup_own, "leaf", 2)
        bulk_low = swapped(bulk_oth[:, :half], "leaf", 2)
        bulk_high = swapped(bulk_far[:, half:], "leaf", 1)
        split = table[: lay.first].reshape(10, lay.per)
        update = plain_merge(
            block_first, split[BOTH:, lay.sep :], split[NODE:BOTH, lay.sep :],
            (coup_own, bulk_oth, bulk_far, bulk_low, bulk_high),
            factors, n_all, rows_of, n_rows,
        )
    return (update[None], window)


def solution(mesh):
    return jax.shard_map(
        per_device,
        mesh=mesh,
        in_specs=(
            P("leaf", None, None),
            P("leaf", "blk", None),
            P(),
            P(),
            P(None, "leaf"),
            P("leaf", "blk"),
        ),
        out_specs=(P("leaf", "blk", None), P("leaf", "blk")),
        check_vma=False,
    )
```

```python
import jax
import jax.numpy as jnp
from jax import lax
from jax.experimental import pallas as pl
from jax.experimental.pallas import tpu as pltpu
from jax.sharding import PartitionSpec as P

BS = 128
SUB = 8
PW = 512
TILE = 512
PIECE = 256
LAST = (((1,), (1,)), ((), ()))
FIRST = (((0,), (0,)), ((), ()))
HIGH = lax.Precision.HIGHEST


def gram(left, right):
    return lax.dot_general(left, right, FIRST, preferred_element_type=jnp.float32)


def outer(left, right):
    return lax.dot_general(left, right, LAST, preferred_element_type=jnp.float32)


def solved(rows, low_inverse):
    return lax.dot_general(
        rows, low_inverse, LAST, precision=HIGH, preferred_element_type=jnp.float32
    )


def exact(left, right):
    return jnp.dot(left, right, precision=HIGH, preferred_element_type=jnp.float32)


def swapped(value, axis, mask):
    return lax.ppermute(value, axis, [(s, s ^ mask) for s in range(lax.axis_size(axis))])


def total(value, axis):
    mask = 1
    while mask < lax.axis_size(axis):
        value = value + swapped(value, axis, mask)
        mask *= 2
    return value


def eliminate_block(block):
    count = BS // SUB
    full = (SUB, BS)
    row_id = lax.broadcasted_iota(jnp.int32, full, 0)
    lane_id = lax.broadcasted_iota(jnp.int32, full, 1)
    t = [block[i * SUB : (i + 1) * SUB, :] for i in range(count)]
    w = [jnp.where(lane_id == row_id + i * SUB, 1.0, 0.0) for i in range(count)]

    def lanes(i, g):
        return [
            jnp.broadcast_to(t[i][:, g * SUB + j : g * SUB + j + 1], full) for j in range(SUB)
        ]

    for g in range(count):
        c = lanes(g, g)
        tg, wg = t[g], w[g]
        row_t, row_w, scale, cross = [], [], [], []
        for j in range(SUB):
            inv = lax.rsqrt(jnp.broadcast_to(c[j][j : j + 1, :], full))
            scale.append(inv)
            row_t.append(jnp.broadcast_to(tg[j : j + 1, :], full) * inv)
            row_w.append(jnp.broadcast_to(wg[j : j + 1, :], full) * inv)
            m = c[j] * inv
            below = {}
            for q in range(j + 1, SUB):
                below[q] = jnp.broadcast_to(m[q : q + 1, :], full)
                c[q] = c[q] - m * below[q]
            cross.append(below)
            if j + 1 < SUB:
                tg = tg - m * row_t[j]
                wg = wg - m * row_w[j]
        out = row_w[0]
        for j in range(1, SUB):
            out = jnp.where(row_id == j, row_w[j], out)
        w[g] = out
        for i in range(g + 1, count):
            c = lanes(i, g)
            for j in range(SUB):
                m = c[j] * scale[j]
                for q in range(j + 1, SUB):
                    c[q] = c[q] - m * cross[j][q]
                t[i] = t[i] - m * row_t[j]
                w[i] = w[i] - m * row_w[j]
    return jnp.concatenate(w, axis=0)


def factor_kernel(block, inverse, rest):
    order = block.shape[0]
    rest[...] = block[...]
    inverse[...] = jnp.zeros_like(inverse)
    for at in range(0, order, BS):
        end = at + BS
        here = eliminate_block(rest[at:end, at:end])
        inverse[at:end, at:end] = here
        if at:
            inverse[at:end, :at] = exact(here, inverse[at:end, :at])
        if end < order:
            panel = exact(here, rest[at:end, end:])
            down = panel.T
            rest[end:, end:] = rest[end:, end:] - exact(down, panel)
            inverse[end:, :end] = inverse[end:, :end] - exact(down, inverse[at:end, :end])


def inverse_factor(block):
    order = block.shape[0]
    return pl.pallas_call(
        factor_kernel,
        out_shape=jax.ShapeDtypeStruct((order, order), jnp.float32),
        in_specs=[pl.BlockSpec(memory_space=pltpu.VMEM)],
        out_specs=pl.BlockSpec(memory_space=pltpu.VMEM),
        scratch_shapes=[pltpu.VMEM((order, order), jnp.float32)],
        compiler_params=pltpu.CompilerParams(vmem_limit_bytes=24 * 2**20),
        cost_estimate=pl.CostEstimate(
            flops=19 * 10**9, bytes_accessed=8 * order**2, transcendentals=0
        ),
    )(block)


def table_kernel(sep_blocks, maps, who, out):
    upd_blocks = maps.shape[1]
    per = sep_blocks + upd_blocks

    def clear(e, _):
        out[e] = -1
        return 0

    lax.fori_loop(0, 10 * per, clear, 0, unroll=8)
    for q in range(6):
        node = who[q]

        def place(i, _, q=q, node=node):
            out[q * per + maps[node, i]] = i
            return 0

        lax.fori_loop(0, upd_blocks, place, 0, unroll=8)
    for q in range(4):

        def chain(e, _, q=q):
            k = out[(4 + q // 2) * per + e]
            got = out[q * per + sep_blocks + jnp.maximum(k, 0)]
            out[(6 + q) * per + e] = jnp.where(k >= 0, got, -1)
            return 0

        lax.fori_loop(0, per, chain, 0, unroll=6)
    for k in range(who.shape[0] - 6):
        out[10 * per + k] = who[6 + k]


def make_table(index_maps, sep_blocks, who):
    entries = 10 * (sep_blocks + index_maps.shape[1]) + who.shape[0] - 6
    return pl.pallas_call(
        lambda maps, who, out: table_kernel(sep_blocks, maps, who, out),
        out_shape=jax.ShapeDtypeStruct((entries,), jnp.int32),
        in_specs=[pl.BlockSpec(memory_space=pltpu.SMEM)] * 2,
        out_specs=pl.BlockSpec(memory_space=pltpu.SMEM),
    )(index_maps, who)


LEAF, NODE, BOTH = 0, 4, 6


class Layout:
    def __init__(self, sep_blocks, upd_blocks):
        self.sep = sep_blocks
        self.per = sep_blocks + upd_blocks
        self.first = 10 * self.per

    def sep_at(self, table, row, s):
        return table[row * self.per + s]

    def upd_at(self, table, row, m):
        return table[row * self.per + self.sep + m]


def block_start(at):
    return pl.multiple_of(jnp.maximum(at, 0) * BS, BS)


def pair_start(at):
    return pl.multiple_of((jnp.maximum(at, 0) % 2) * BS, BS)


def kept(keep, value):
    return jnp.where(keep, value, jnp.zeros_like(value))


def extract_kernel(lay, table, coup, c1, s1, c2, s2):
    step = pl.program_id(0)
    group = table[lay.first] // 2 + step

    @pl.when(step == 0)
    def _():
        s1[...] = jnp.zeros_like(s1)
        s2[...] = jnp.zeros_like(s2)

    for row, below, pivot in ((LEAF, c1, s1), (BOTH, c2, s2)):
        for s in range(lay.sep):
            col = lay.sep_at(table, row, s)
            cols = pl.ds(block_start(col), BS)
            at = slice(s * BS, (s + 1) * BS)
            for h in range(2):
                src = lay.upd_at(table, row, 2 * group + h)
                got = coup[pl.ds(pair_start(src), BS), cols]
                below[h * BS : (h + 1) * BS, at] = kept((src >= 0) & (col >= 0), got)
            for r in range(lay.sep):
                src = lay.sep_at(table, row, r)

                @pl.when((src >= 0) & (src // 2 == group))
                def _(src=src, r=r, at=at, cols=cols, col=col, pivot=pivot):
                    got = coup[pl.ds(pair_start(src), BS), cols]
                    pivot[r * BS : (r + 1) * BS, at] = kept(col >= 0, got)


def extract(lay, table, coup):
    rows, width = coup.shape
    sep = lay.sep * BS
    below = jax.ShapeDtypeStruct((rows, sep), coup.dtype)
    pivot = jax.ShapeDtypeStruct((sep, sep), coup.dtype)
    strip = pl.BlockSpec((2 * BS, sep), lambda i: (i, 0))
    fixed = pl.BlockSpec((sep, sep), lambda i: (0, 0))
    return pl.pallas_call(
        lambda *refs: extract_kernel(lay, *refs),
        grid=(rows // (2 * BS),),
        out_shape=(below, pivot, below, pivot),
        in_specs=[
            pl.BlockSpec(memory_space=pltpu.SMEM),
            pl.BlockSpec((2 * BS, width), lambda i: (i, 0)),
        ],
        out_specs=(strip, fixed, strip, fixed),
        compiler_params=pltpu.CompilerParams(vmem_limit_bytes=24 * 2**20),
    )(table, coup)


def pick_kernel(picks, table, *refs):
    nets, out = refs[:-1], refs[-1]
    depth = nets[0].shape[0]
    for q, net in enumerate(nets):
        for k, pick in enumerate(picks):
            at = pick(table, q)
            out[q * depth : (q + 1) * depth, k * BS : (k + 1) * BS] = kept(
                at >= 0, net[:, pl.ds(block_start(at), BS)]
            )


def pick_columns(picks, table, nets):
    return pl.pallas_call(
        lambda *refs: pick_kernel(picks, *refs),
        out_shape=jax.ShapeDtypeStruct(
            (len(nets) * nets[0].shape[0], len(picks) * BS), nets[0].dtype
        ),
        in_specs=[pl.BlockSpec(memory_space=pltpu.SMEM)]
        + [pl.BlockSpec(memory_space=pltpu.VMEM)] * len(nets),
        out_specs=pl.BlockSpec(memory_space=pltpu.VMEM),
        compiler_params=pltpu.CompilerParams(vmem_limit_bytes=24 * 2**20),
    )(table, *nets)


def front_kernel(lay, table, l_row, far_row, l_sep, far_sep, n_rows, n_sep, *refs):
    coups, (below, r_own, r_far) = refs[:-3], refs[-3:]
    group = table[lay.first] // 2 + pl.program_id(0)
    for p, row, out in ((0, l_row, r_own), (1, far_row, r_far)):
        for h in range(2):
            src = lay.upd_at(table, NODE + p, 2 * group + h)
            out[h * BS : (h + 1) * BS, :] = kept(src >= 0, row[pl.ds(pair_start(src), BS), :])
    value = jnp.dot(n_rows[...], n_sep[...], preferred_element_type=jnp.float32)
    for ref in coups:
        value = value + ref[...].astype(jnp.float32)
    value = value - outer(r_own[...], l_sep[...])
    below[...] = value - outer(r_far[...], far_sep[...])


def front(lay, table, l_row, far_row, l_sep, far_sep, n_rows, n_sep, coups):
    rows, sep = l_row.shape
    nets = n_rows.shape[1]
    strip = pl.BlockSpec((2 * BS, sep), lambda i: (i, 0))
    fixed = pl.BlockSpec((sep, sep), lambda i: (0, 0))
    picked = jax.ShapeDtypeStruct((rows, sep), l_row.dtype)
    return pl.pallas_call(
        lambda *refs: front_kernel(lay, *refs),
        grid=(rows // (2 * BS),),
        out_shape=(jax.ShapeDtypeStruct((rows, sep), jnp.float32), picked, picked),
        in_specs=[
            pl.BlockSpec(memory_space=pltpu.SMEM),
            strip,
            strip,
            fixed,
            fixed,
            pl.BlockSpec((2 * BS, nets), lambda i: (i, 0)),
            pl.BlockSpec((nets, sep), lambda i: (0, 0)),
        ]
        + [strip] * len(coups),
        out_specs=(strip, strip, strip),
        compiler_params=pltpu.CompilerParams(vmem_limit_bytes=24 * 2**20),
    )(table, l_row, far_row, l_sep, far_sep, n_rows, n_sep, *coups)


def copy_kernel(table, rows, out):
    out[...] = rows[...]


def pick_rows(lay, table, row, rows):
    width = rows.shape[1]
    spec = pltpu.PrefetchScalarGridSpec(
        num_scalar_prefetch=1,
        grid=(lay.sep,),
        in_specs=[
            pl.BlockSpec((BS, width), lambda i, t: (jnp.maximum(t[row * lay.per + i], 0), 0))
        ],
        out_specs=pl.BlockSpec((BS, width), lambda i, t: (i, 0)),
    )
    return pl.pallas_call(
        copy_kernel,
        out_shape=jax.ShapeDtypeStruct((lay.sep * BS, width), rows.dtype),
        grid_spec=spec,
    )(table, rows)


def merge_kernel(
    lay, table, own, *refs
):
    bulk = refs[:15]
    (l_own, l_far, l_new, n_all, r_own, r_far, r_new, n_rows, out) = refs[15:24]
    left, right, turn, turned = refs[24:]
    rows, tile = out.shape
    sep = l_own.shape[1]
    step = pl.program_id(0)
    kind, side = step // 2, step % 2
    first_row = table[lay.first]
    col_tile = (table[lay.first + 1 + kind] * 2 + side) * (tile // BS)
    even = table[lay.first] // (rows // BS) % 2 == 0
    others = (1, 2, 3)

    @pl.when(step == 0)
    def _():
        left[:, :sep] = -r_own[...]
        left[:, sep : 2 * sep] = -r_far[...]
        left[:, 2 * sep : 3 * sep] = -r_new[...]
        left[:, 3 * sep :] = n_rows[...]
        lane = lax.broadcasted_iota(jnp.int32, (BS, 2 * BS), 1)
        row = lax.broadcasted_iota(jnp.int32, (BS, 2 * BS), 0)
        for r in range(rows // BS):
            for n, q in enumerate(others):
                at = lay.upd_at(table, BOTH + q, first_row + r)
                hit = (lane == row + pair_start(at)) & (at >= 0)
                turn[r * BS : (r + 1) * BS, n * PIECE : (n + 1) * PIECE] = jnp.where(
                    hit, 1.0, 0.0
                ).astype(jnp.bfloat16)

    def col_of(piece, c):
        return col_tile + piece * 2 + c

    def add(ref, q, r, piece, c, value):
        row_at = lay.upd_at(table, BOTH + q, first_row + r)
        col_at = lay.upd_at(table, BOTH + q, col_of(piece, c))
        row_off = pl.multiple_of(pair_start(row_at) + (r // 2) * 2 * BS, BS)
        col_off = pl.multiple_of(pair_start(col_at) + piece * PIECE, BS)
        got = ref[pl.ds(row_off, BS), pl.ds(col_off, BS)].astype(jnp.float32)
        return value + jnp.where((row_at >= 0) & (col_at >= 0), got, 0.0)

    for piece in range(tile // PIECE):
        for p, ref in ((0, l_own), (1, l_far)):
            for c in range(2):
                at = lay.upd_at(table, NODE + p, col_of(piece, c))
                off = pl.multiple_of(pair_start(at) + piece * PIECE, BS)
                right[c * BS : (c + 1) * BS, p * sep : (p + 1) * sep] = kept(
                    at >= 0, ref[pl.ds(off, BS), :]
                )
        cols = slice(piece * PIECE, (piece + 1) * PIECE)
        right[:, 2 * sep : 3 * sep] = l_new[cols, :]
        right[:, 3 * sep :] = n_all[cols, :]
        for r in range(0, rows // BS, 2):
            prod = outer(left[r * BS : (r + 2) * BS, :], right[...])
            for h in range(2):
                for c in range(2):
                    value = prod[h * BS : (h + 1) * BS, c * BS : (c + 1) * BS]
                    at = piece * PIECE + c * BS
                    out[(r + h) * BS : (r + h + 1) * BS, at : at + BS] = add(
                        own, 0, r + h, piece, c, value
                    )

    def direct(sources):
        for piece in range(tile // PIECE):
            for r in range(rows // BS):
                for c in range(2):
                    spot = (
                        slice(r * BS, (r + 1) * BS),
                        slice(piece * PIECE + c * BS, piece * PIECE + (c + 1) * BS),
                    )
                    value = out[spot]
                    for q, ref in zip(others, sources):
                        value = add(ref, q, r, piece, c, value)
                    out[spot] = value

    def transposed(sources):
        width = len(others) * PIECE
        for piece in range(tile // PIECE):
            for c in range(2):
                for n, (q, ref) in enumerate(zip(others, sources)):
                    at = lay.upd_at(table, BOTH + q, col_of(piece, c))
                    off = pl.multiple_of(pair_start(at) + piece * PIECE, BS)
                    got = kept(at >= 0, ref[pl.ds(off, BS), :])
                    for g in range(rows // PIECE):
                        to = g * width + n * PIECE
                        turned[c * BS : (c + 1) * BS, to : to + PIECE] = got[
                            :, g * PIECE : (g + 1) * PIECE
                        ]
            cols = slice(piece * PIECE, (piece + 1) * PIECE)
            for g in range(rows // PIECE):
                spot = slice(g * PIECE, (g + 1) * PIECE)
                out[spot, cols] = out[spot, cols] + outer(
                    turn[spot, :], turned[:, g * width : (g + 1) * width]
                )

    for case, run, at in (
        (kind == 0, direct, 0),
        (kind == 1, direct, 3),
        (kind == 2, transposed, 6),
        ((kind == 3) & even, direct, 9),
        ((kind == 3) & jnp.logical_not(even), transposed, 12),
    ):

        @pl.when(case)
        def _(run=run, at=at):
            run(bulk[at : at + 3])


def merge(lay, table, own, diag, follow, turned, extra, extra_turned, factors, n_all, rows_of, n_rows):
    rows, cols = own.shape
    sep = factors[0].shape[1]
    nets = n_all.shape[1]
    depth = 3 * sep + nets
    strip_at = lambda i, t: t[lay.first + 1 + i // 2] * 2 + i % 2
    once = pl.Buffered(1)
    whole = lambda width: pl.BlockSpec((rows, width), lambda i, t: (0, 0), pipeline_mode=once)
    strip = lambda width: pl.BlockSpec((TILE, width), lambda i, t: (strip_at(i, t), 0))
    tile = pl.BlockSpec((rows, TILE), lambda i, t: (0, strip_at(i, t)))

    def wide(k):
        return pl.BlockSpec((rows, TILE), lambda i, t: (0, jnp.clip(i - 2 * k, 0, 1)))

    def tall(k):
        return pl.BlockSpec((TILE, rows), lambda i, t: (jnp.clip(i - 2 * k, 0, 1), 0))

    spec = pltpu.PrefetchScalarGridSpec(
        num_scalar_prefetch=1,
        grid=(cols // TILE,),
        in_specs=[tile]
        + [wide(0)] * 3
        + [wide(1)] * 3
        + [tall(2)] * 3
        + [wide(3)] * 3
        + [tall(3)] * 3
        + [strip(sep)] * 3
        + [strip(nets)]
        + [whole(sep)] * 3
        + [whole(nets)],
        out_specs=tile,
        scratch_shapes=[
            pltpu.VMEM((rows, depth), jnp.bfloat16),
            pltpu.VMEM((PIECE, depth), jnp.bfloat16),
            pltpu.VMEM((rows, 3 * PIECE), jnp.bfloat16),
            pltpu.VMEM((PIECE, 3 * rows), jnp.bfloat16),
        ],
    )
    return pl.pallas_call(
        lambda *refs: merge_kernel(lay, *refs),
        out_shape=jax.ShapeDtypeStruct((rows, cols), jnp.float32),
        grid_spec=spec,
        compiler_params=pltpu.CompilerParams(vmem_limit_bytes=56 * 2**20),
        cost_estimate=pl.CostEstimate(
            flops=2 * rows * cols * depth,
            bytes_accessed=12 * rows * cols + 2 * cols * depth,
            transcendentals=0,
        ),
    )(
        table, own, *diag, *follow, *turned, *extra, *extra_turned, *factors, n_all, *rows_of, n_rows
    )


def plain_merge_kernel(
    table, own, oth, far, low, high, l_own, l_far, l_new, n_all,
    r_own, r_far, r_new, n_rows, out, left, right,
):
    rows, tile = out.shape
    sep = l_own.shape[1]
    step = pl.program_id(0)
    half = pl.num_programs(0) // 2
    per = (table.shape[0] - 1) // 6
    first_row = table[6 * per]

    @pl.when(step == 0)
    def _():
        left[:, :sep] = -r_own[...]
        left[:, sep : 2 * sep] = -r_far[...]
        left[:, 2 * sep : 3 * sep] = -r_new[...]
        left[:, 3 * sep :] = n_rows[...]

    def spot(kind, block):
        at = table[kind * per + block]
        return at, pl.multiple_of((jnp.maximum(at, 0) % 2) * BS, BS)

    def add(ref, kind, r, piece, c, value):
        row_at, row_off = spot(kind, first_row + r)
        col_at, col_off = spot(kind, step * (tile // BS) + piece * 2 + c)
        row_off = pl.multiple_of(row_off + (r // 2) * 2 * BS, BS)
        col_off = pl.multiple_of(col_off + piece * PIECE, BS)
        got = ref[pl.ds(row_off, BS), pl.ds(col_off, BS)].astype(jnp.float32)
        return value + jnp.where((row_at >= 0) & (col_at >= 0), got, 0.0)

    for piece in range(tile // PIECE):
        for kind, ref in ((4, l_own), (5, l_far)):
            for c in range(2):
                at, off = spot(kind, step * (tile // BS) + piece * 2 + c)
                off = pl.multiple_of(off + piece * PIECE, BS)
                got = ref[pl.ds(off, BS), :]
                right[c * BS : (c + 1) * BS, (kind - 4) * sep : (kind - 3) * sep] = jnp.where(
                    at >= 0, got, jnp.zeros_like(got)
                )
        cols = slice(piece * PIECE, (piece + 1) * PIECE)
        right[:, 2 * sep : 3 * sep] = l_new[cols, :]
        right[:, 3 * sep :] = n_all[cols, :]
        for r in range(0, rows // BS, 2):
            prod = outer(left[r * BS : (r + 2) * BS, :], right[...])
            for h in range(2):
                for c in range(2):
                    value = prod[h * BS : (h + 1) * BS, c * BS : (c + 1) * BS]
                    for kind, ref in ((0, own), (1, oth), (2, far)):
                        value = add(ref, kind, r + h, piece, c, value)
                    at = piece * PIECE + c * BS
                    out[(r + h) * BS : (r + h + 1) * BS, at : at + BS] = value

    for side, ref in ((step < half, low), (step >= half, high)):

        @pl.when(side)
        def _(ref=ref):
            for piece in range(tile // PIECE):
                for r in range(rows // BS):
                    for c in range(2):
                        at = piece * PIECE + c * BS
                        spot_rows = slice(r * BS, (r + 1) * BS)
                        out[spot_rows, at : at + BS] = add(
                            ref, 3, r, piece, c, out[spot_rows, at : at + BS]
                        )


def plain_merge(block_first, comp, node_upd, coups, factors, n_all, rows_of, n_rows):
    own, oth, far, low, high = coups
    rows, cols = own.shape
    sep = factors[0].shape[1]
    nets = n_all.shape[1]
    steps = cols // TILE
    half = steps // 2
    table = jnp.concatenate(
        [comp.reshape(-1), node_upd.reshape(-1), jnp.int32(block_first)[None]]
    )
    depth = 3 * sep + nets
    whole = lambda width: pl.BlockSpec((rows, width), lambda i: (0, 0))
    strip = lambda width: pl.BlockSpec((TILE, width), lambda i: (i, 0))
    tile = pl.BlockSpec((rows, TILE), lambda i: (0, i))
    return pl.pallas_call(
        plain_merge_kernel,
        grid=(steps,),
        out_shape=jax.ShapeDtypeStruct((rows, cols), jnp.float32),
        in_specs=[
            pl.BlockSpec(memory_space=pltpu.SMEM),
            tile,
            tile,
            tile,
            pl.BlockSpec((rows, TILE), lambda i: (0, jnp.minimum(i, half - 1))),
            pl.BlockSpec((rows, TILE), lambda i: (0, jnp.maximum(i - half, 0))),
            strip(sep),
            strip(sep),
            strip(sep),
            strip(nets),
            whole(sep),
            whole(sep),
            whole(sep),
            whole(nets),
        ],
        out_specs=pl.BlockSpec((rows, TILE), lambda i: (0, i)),
        scratch_shapes=[
            pltpu.VMEM((rows, depth), jnp.bfloat16),
            pltpu.VMEM((PIECE, depth), jnp.bfloat16),
        ],
        compiler_params=pltpu.CompilerParams(vmem_limit_bytes=52 * 2**20),
        cost_estimate=pl.CostEstimate(
            flops=2 * rows * cols * depth,
            bytes_accessed=12 * rows * cols + 2 * cols * depth,
            transcendentals=0,
        ),
    )(table, own, oth, far, low, high, *factors, n_all, *rows_of, n_rows)


def leaf_spread(value, source_of, step):
    leaf_count, blk_count = lax.axis_size("leaf"), lax.axis_size("blk")
    sources = jnp.array([source_of(b) for b in range(blk_count)], jnp.int32)
    rank = lax.axis_index("leaf") ^ sources[lax.axis_index("blk")]
    pairs = []
    for b in range(blk_count):
        for r in range(0, leaf_count, 2 * step):
            src = source_of(b)
            pairs.append(((r ^ src) * blk_count + b, ((r + step) ^ src) * blk_count + b))
    got = lax.ppermute(value, ("leaf", "blk"), pairs)
    return jnp.where(rank % (2 * step) == step, got, value)


def first_two_far(value):
    blk_count = lax.axis_size("blk")
    blk_pos = lax.axis_index("blk")
    step = 2
    while step < blk_count:
        got = lax.ppermute(value, "blk", [(s, s + step) for s in range(step)])
        value = jnp.where((blk_pos >= step) & (blk_pos < 2 * step), got, value)
        step *= 2
    return value


def first_two_near(value):
    mate = swapped(value, "blk", 1)
    even = lax.axis_index("blk") % 2 == 0
    return jnp.where(even, value, mate), jnp.where(even, mate, value)


class Link:
    def __init__(self):
        self.last = None

    def __call__(self, send, value):
        if self.last is not None:
            value, _ = lax.optimization_barrier((value, self.last))
        self.last = send(value)
        return self.last


def per_device(leaf_net, leaf_coupling, index_maps, sep_anchor, top_net, top_coupling):
    leaf_count, blk_count = lax.axis_size("leaf"), lax.axis_size("blk")
    leaf_pos, blk_pos = lax.axis_index("leaf"), lax.axis_index("blk")
    net_own = leaf_net[0]
    coup_own = leaf_coupling[0]
    rows_dev, upd_order = coup_own.shape
    sep_order = sep_anchor.shape[1]
    block_rows = rows_dev // BS
    lay = Layout(sep_order // BS, upd_order // BS)
    block_first = blk_pos * block_rows
    node = leaf_pos >> 1
    triangle = blk_count == 4
    f32 = lambda value: value.astype(jnp.float32)
    tie = lax.optimization_barrier

    def among(options):
        return jnp.array(options, jnp.int32)[blk_pos]

    follow_to = (2, 3, 1, 0)
    places = [block_first]
    if triangle:
        places += [blk_pos, among(follow_to), among((3, 2, 0, 1)), blk_pos ^ 1]
    who = [leaf_pos ^ q for q in range(4)] + [leaf_count + node, leaf_count + (node ^ 1)]
    table = make_table(index_maps, lay.sep, jnp.stack(who + places))

    lead = 2 * PW
    rows_top = top_net.shape[1]
    same_source = blk_count * PW <= rows_top

    def spread(values, step):
        if same_source:
            return (leaf_spread(values[0], lambda b: 0, step),)
        return (
            leaf_spread(values[0], lambda b: 0, step),
            leaf_spread(values[1], lambda b: (b * PW) // rows_top, step),
        )

    piece = lax.dynamic_slice_in_dim(top_net, (blk_pos * PW) % rows_top, PW, 1)
    ours = (top_coupling[:lead], piece)
    if same_source:
        ours = (jnp.concatenate(ours, axis=0),)

    def leaf_even(mask):
        pairs = [
            (l * blk_count + b, (l ^ mask) * blk_count + b)
            for l in range(leaf_count)
            for b in range(0, blk_count, 2)
        ]
        return lambda value: lax.ppermute(value, ("leaf", "blk"), pairs)

    def turn(value):
        return lax.ppermute(value, "blk", [(b, follow_to[b]) for b in range(blk_count)])

    def to_odd(value):
        return lax.ppermute(value, "blk", [(b, b + 1) for b in range(0, blk_count, 2)])

    def block(src, c):
        return lax.dynamic_slice_in_dim(src, c * rows_dev, rows_dev, 1)

    across_y, across_z, across_x = Link(), Link(), Link()
    near = lambda value: across_y(lambda v: swapped(v, "leaf", 1), value)
    far = lambda value: across_z(lambda v: swapped(v, "leaf", 2), value)

    net_oth = near(net_own)
    c1_own, s1, c2_own, s2 = extract(lay, table, coup_own)
    s1_own = across_x(lambda v: total(v, "blk"), s1)
    s1_oth = near(s1_own)
    ours, _ = tie((ours, table))
    step = leaf_count // 2
    while step >= 4:
        ours = across_z(lambda v: spread(v, step), ours)
        step //= 2
    c2_far = far(c2_own)
    ours = across_z(lambda v: spread(v, 2), ours)
    net_far = far(jnp.concatenate([net_own, net_oth], axis=1))
    net_far, net_far_oth = net_far[:, :upd_order], net_far[:, upd_order:]
    s2_own = across_x(lambda v: total(v, "blk"), s2)
    c1_oth, s2_oth = near(c1_own), near(s2_own)
    c2_oth, c2_far_oth = near(c2_own), near(c2_far)
    ours = across_y(lambda v: spread(v, 1), ours)
    s2_far = far(jnp.concatenate([s2_own, s2_oth], axis=1))
    s2_far, s2_far_oth = s2_far[:, :sep_order], s2_far[:, sep_order:]

    pick1 = [lambda t, q, s=s: lay.sep_at(t, LEAF + q, s) for s in range(lay.sep)]
    pick1 += [
        lambda t, q, i=i: lay.upd_at(t, LEAF + q, t[lay.first] + i) for i in range(block_rows)
    ]
    n1 = pick_columns(pick1, table, [net_own, net_oth])
    n1_sep, n1_rows = n1[:, :sep_order], n1[:, sep_order:]
    pivot = gram(n1_sep, n1_sep) + f32(s1_own) + f32(s1_oth) + jnp.diag(sep_anchor[node])
    low1 = inverse_factor(pivot)
    below = gram(n1_rows, n1_sep) + f32(c1_own) + f32(c1_oth)
    lrow1 = solved(below, low1).astype(jnp.bfloat16)
    l_own = lax.all_gather(lrow1, "blk", axis=0, tiled=True)
    lrow1_far = far(lrow1)
    l_sep = pick_rows(lay, table, NODE, l_own)
    l_sep_far = far(l_sep)

    if same_source:
        lead_mine, net_mine = ours[0][:lead], ours[0][lead:]
        both0, both1 = first_two_near(across_x(first_two_far, ours[0]))
    else:
        lead_mine, net_mine = ours
        both0, both1 = first_two_near(
            across_x(first_two_far, jnp.concatenate(ours, axis=0))
        )
    coup_even_odd = across_x(first_two_far, top_coupling)
    l_far = lax.all_gather(lrow1_far, "blk", axis=0, tiled=True)

    if triangle:
        follow0 = block(coup_own, among(follow_to))
        diag0, extra0 = block(coup_own, blk_pos), block(coup_own, blk_pos ^ 1)
        follow1, follow2 = near(follow0), far(follow0)

    pick2 = [lambda t, q, s=s: lay.sep_at(t, BOTH + q, s) for s in range(lay.sep)]
    pick2 += [lambda t, q, m=m: lay.upd_at(t, BOTH + q, m) for m in range(upd_order // BS)]
    n2 = pick_columns(pick2, table, [net_own, net_oth, net_far, net_far_oth])
    n2_sep = n2[:, :sep_order]
    n_all = n2[:, sep_order:].T
    n_rows = lax.dynamic_slice_in_dim(n_all, blk_pos * rows_dev, rows_dev, 0)

    below, r_own, r_far = front(
        lay, table, lrow1, lrow1_far, l_sep, l_sep_far, n_rows, n2_sep,
        (c2_own, c2_oth, c2_far, c2_far_oth),
    )
    pivot = gram(n2_sep, n2_sep) + f32(s2_own) + f32(s2_oth) + f32(s2_far) + f32(s2_far_oth)
    pivot = pivot - outer(l_sep, l_sep) - outer(l_sep_far, l_sep_far)
    low2 = inverse_factor(pivot + jnp.diag(sep_anchor[leaf_count // 2 + (node >> 1)]))
    r_new = solved(below, low2).astype(jnp.bfloat16)
    l_new = lax.all_gather(r_new, "blk", axis=0, tiled=True)

    if triangle:
        r_new, follow1, follow2, both0, both1 = tie((r_new, follow1, follow2, both0, both1))
        diag1, follow3 = near(diag0), far(follow1)
        turned1 = across_x(turn, follow1)
        extra1, diag2 = across_y(leaf_even(1), extra0), far(diag0)
        turned2 = across_x(turn, follow2)
        extra2 = across_z(leaf_even(2), extra0)
        diag3 = near(diag2)
        turned3 = across_x(turn, follow3)
        extra3 = across_y(leaf_even(1), extra2)
        low_extra1, low_extra2, low_extra3 = to_odd(extra1), to_odd(extra2), to_odd(extra3)

    coup0, coup1 = first_two_near(coup_even_odd)
    lead0, net0 = f32(both0[:lead]), both0[lead:]
    lead1, net1 = f32(both1[:lead]), both1[lead:]
    mine = f32(lead_mine)
    inv0 = inverse_factor(gram(net0, net0) + lead0[:PW])
    cross = solved(gram(net1, net0) + lead0[PW:], inv0).astype(jnp.bfloat16)
    inv1 = inverse_factor(gram(net1, net1) + lead1[PW:] - outer(cross, cross))

    row = (leaf_pos * rows_top + jnp.arange(rows_top, dtype=jnp.int32))[:, None]
    col = jnp.arange(PW, dtype=jnp.int32)[None, :]

    def panel(current, low, first):
        return jnp.where(row - first >= col, solved(current, low), 0.0)

    q0 = solved((gram(net0, net_mine) + mine[:PW]).T, inv0).astype(jnp.bfloat16)
    q1 = solved((gram(net1, net_mine) + mine[PW:]).T - outer(q0, cross), inv1)
    q1 = q1.astype(jnp.bfloat16)
    p0 = panel(gram(top_net, net0) + f32(coup0), inv0, 0)
    b0 = p0.astype(jnp.bfloat16)
    x1 = gram(top_net, net1) + f32(coup1) - outer(b0, cross)
    p1 = panel(x1, inv1, PW)
    rest = gram(top_net, net_mine) + f32(top_coupling) - outer(b0, q0)
    rest = rest - outer(p1.astype(jnp.bfloat16), q1)
    window = jnp.where(blk_pos == 0, p0, jnp.where(blk_pos == 1, p1, rest))

    factors, rows_of = (l_own, l_far, l_new), (r_own, r_far, r_new)
    if triangle:
        update = merge(
            lay, table, coup_own,
            (diag1, diag2, diag3),
            (follow1, follow2, follow3),
            (turned1, turned2, turned3),
            (extra1, extra2, extra3),
            (low_extra1, low_extra2, low_extra3),
            factors, n_all, rows_of, n_rows,
        )
    else:
        half = upd_order // 2
        bulk_oth, bulk_far = swapped(coup_own, "leaf", 1), swapped(coup_own, "leaf", 2)
        bulk_low = swapped(bulk_oth[:, :half], "leaf", 2)
        bulk_high = swapped(bulk_far[:, half:], "leaf", 1)
        split = table[: lay.first].reshape(10, lay.per)
        update = plain_merge(
            block_first, split[BOTH:, lay.sep :], split[NODE:BOTH, lay.sep :],
            (coup_own, bulk_oth, bulk_far, bulk_low, bulk_high),
            factors, n_all, rows_of, n_rows,
        )
    return (update[None], window)


def solution(mesh):
    return jax.shard_map(
        per_device,
        mesh=mesh,
        in_specs=(
            P("leaf", None, None),
            P("leaf", "blk", None),
            P(),
            P(),
            P(None, "leaf"),
            P("leaf", "blk"),
        ),
        out_specs=(P("leaf", "blk", None), P("leaf", "blk")),
        check_vma=False,
    )
```

```python
import jax
import jax.numpy as jnp
from jax import lax
from jax.experimental import pallas as pl
from jax.experimental.pallas import tpu as pltpu
from jax.sharding import PartitionSpec as P

BS = 128
SUB = 8
PW = 512
TILE = 512
PIECE = 256
LAST = (((1,), (1,)), ((), ()))
FIRST = (((0,), (0,)), ((), ()))
HIGH = lax.Precision.HIGHEST


def gram(left, right):
    return lax.dot_general(left, right, FIRST, preferred_element_type=jnp.float32)


def outer(left, right):
    return lax.dot_general(left, right, LAST, preferred_element_type=jnp.float32)


def solved(rows, low_inverse):
    return lax.dot_general(
        rows, low_inverse, LAST, precision=HIGH, preferred_element_type=jnp.float32
    )


def exact(left, right):
    return jnp.dot(left, right, precision=HIGH, preferred_element_type=jnp.float32)


def swapped(value, axis, mask):
    return lax.ppermute(value, axis, [(s, s ^ mask) for s in range(lax.axis_size(axis))])


def total(value, axis):
    mask = 1
    while mask < lax.axis_size(axis):
        value = value + swapped(value, axis, mask)
        mask *= 2
    return value


def eliminate_block(block):
    count = BS // SUB
    full = (SUB, BS)
    row_id = lax.broadcasted_iota(jnp.int32, full, 0)
    lane_id = lax.broadcasted_iota(jnp.int32, full, 1)
    t = [block[i * SUB : (i + 1) * SUB, :] for i in range(count)]
    w = [jnp.where(lane_id == row_id + i * SUB, 1.0, 0.0) for i in range(count)]

    def lanes(i, g):
        return [
            jnp.broadcast_to(t[i][:, g * SUB + j : g * SUB + j + 1], full) for j in range(SUB)
        ]

    for g in range(count):
        c = lanes(g, g)
        tg, wg = t[g], w[g]
        row_t, row_w, scale, cross = [], [], [], []
        for j in range(SUB):
            inv = lax.rsqrt(jnp.broadcast_to(c[j][j : j + 1, :], full))
            scale.append(inv)
            row_t.append(jnp.broadcast_to(tg[j : j + 1, :], full) * inv)
            row_w.append(jnp.broadcast_to(wg[j : j + 1, :], full) * inv)
            m = c[j] * inv
            below = {}
            for q in range(j + 1, SUB):
                below[q] = jnp.broadcast_to(m[q : q + 1, :], full)
                c[q] = c[q] - m * below[q]
            cross.append(below)
            if j + 1 < SUB:
                tg = tg - m * row_t[j]
                wg = wg - m * row_w[j]
        out = row_w[0]
        for j in range(1, SUB):
            out = jnp.where(row_id == j, row_w[j], out)
        w[g] = out
        for i in range(g + 1, count):
            c = lanes(i, g)
            for j in range(SUB):
                m = c[j] * scale[j]
                for q in range(j + 1, SUB):
                    c[q] = c[q] - m * cross[j][q]
                t[i] = t[i] - m * row_t[j]
                w[i] = w[i] - m * row_w[j]
    return jnp.concatenate(w, axis=0)


def factor_kernel(block, inverse, rest):
    order = block.shape[0]
    rest[...] = block[...]
    inverse[...] = jnp.zeros_like(inverse)
    for at in range(0, order, BS):
        end = at + BS
        here = eliminate_block(rest[at:end, at:end])
        inverse[at:end, at:end] = here
        if at:
            inverse[at:end, :at] = exact(here, inverse[at:end, :at])
        if end < order:
            panel = exact(here, rest[at:end, end:])
            down = panel.T
            rest[end:, end:] = rest[end:, end:] - exact(down, panel)
            inverse[end:, :end] = inverse[end:, :end] - exact(down, inverse[at:end, :end])


def inverse_factor(block):
    order = block.shape[0]
    return pl.pallas_call(
        factor_kernel,
        out_shape=jax.ShapeDtypeStruct((order, order), jnp.float32),
        in_specs=[pl.BlockSpec(memory_space=pltpu.VMEM)],
        out_specs=pl.BlockSpec(memory_space=pltpu.VMEM),
        scratch_shapes=[pltpu.VMEM((order, order), jnp.float32)],
        compiler_params=pltpu.CompilerParams(vmem_limit_bytes=24 * 2**20),
        cost_estimate=pl.CostEstimate(
            flops=19 * 10**9, bytes_accessed=8 * order**2, transcendentals=0
        ),
    )(block)


def table_kernel(sep_blocks, maps, who, out):
    upd_blocks = maps.shape[1]
    per = sep_blocks + upd_blocks

    def clear(e, _):
        out[e] = -1
        return 0

    lax.fori_loop(0, 10 * per, clear, 0, unroll=8)
    for q in range(6):
        node = who[q]

        def place(i, _, q=q, node=node):
            out[q * per + maps[node, i]] = i
            return 0

        lax.fori_loop(0, upd_blocks, place, 0, unroll=8)
    for q in range(4):

        def chain(e, _, q=q):
            k = out[(4 + q // 2) * per + e]
            got = out[q * per + sep_blocks + jnp.maximum(k, 0)]
            out[(6 + q) * per + e] = jnp.where(k >= 0, got, -1)
            return 0

        lax.fori_loop(0, per, chain, 0, unroll=6)
    for k in range(who.shape[0] - 6):
        out[10 * per + k] = who[6 + k]


def make_table(index_maps, sep_blocks, who):
    entries = 10 * (sep_blocks + index_maps.shape[1]) + who.shape[0] - 6
    return pl.pallas_call(
        lambda maps, who, out: table_kernel(sep_blocks, maps, who, out),
        out_shape=jax.ShapeDtypeStruct((entries,), jnp.int32),
        in_specs=[pl.BlockSpec(memory_space=pltpu.SMEM)] * 2,
        out_specs=pl.BlockSpec(memory_space=pltpu.SMEM),
    )(index_maps, who)


LEAF, NODE, BOTH = 0, 4, 6


class Layout:
    def __init__(self, sep_blocks, upd_blocks):
        self.sep = sep_blocks
        self.per = sep_blocks + upd_blocks
        self.first = 10 * self.per

    def sep_at(self, table, row, s):
        return table[row * self.per + s]

    def upd_at(self, table, row, m):
        return table[row * self.per + self.sep + m]


def block_start(at):
    return pl.multiple_of(jnp.maximum(at, 0) * BS, BS)


def pair_start(at):
    return pl.multiple_of((jnp.maximum(at, 0) % 2) * BS, BS)


def kept(keep, value):
    return jnp.where(keep, value, jnp.zeros_like(value))


def extract_kernel(lay, table, coup, c1, s1, c2, s2):
    step = pl.program_id(0)
    group = table[lay.first] // 2 + step

    @pl.when(step == 0)
    def _():
        s1[...] = jnp.zeros_like(s1)
        s2[...] = jnp.zeros_like(s2)

    for row, below, pivot in ((LEAF, c1, s1), (BOTH, c2, s2)):
        for s in range(lay.sep):
            col = lay.sep_at(table, row, s)
            cols = pl.ds(block_start(col), BS)
            at = slice(s * BS, (s + 1) * BS)
            for h in range(2):
                src = lay.upd_at(table, row, 2 * group + h)
                got = coup[pl.ds(pair_start(src), BS), cols]
                below[h * BS : (h + 1) * BS, at] = kept((src >= 0) & (col >= 0), got)
            for r in range(lay.sep):
                src = lay.sep_at(table, row, r)

                @pl.when((src >= 0) & (src // 2 == group))
                def _(src=src, r=r, at=at, cols=cols, col=col, pivot=pivot):
                    got = coup[pl.ds(pair_start(src), BS), cols]
                    pivot[r * BS : (r + 1) * BS, at] = kept(col >= 0, got)


def extract(lay, table, coup):
    rows, width = coup.shape
    sep = lay.sep * BS
    below = jax.ShapeDtypeStruct((rows, sep), coup.dtype)
    pivot = jax.ShapeDtypeStruct((sep, sep), coup.dtype)
    strip = pl.BlockSpec((2 * BS, sep), lambda i: (i, 0))
    fixed = pl.BlockSpec((sep, sep), lambda i: (0, 0))
    return pl.pallas_call(
        lambda *refs: extract_kernel(lay, *refs),
        grid=(rows // (2 * BS),),
        out_shape=(below, pivot, below, pivot),
        in_specs=[
            pl.BlockSpec(memory_space=pltpu.SMEM),
            pl.BlockSpec((2 * BS, width), lambda i: (i, 0)),
        ],
        out_specs=(strip, fixed, strip, fixed),
        compiler_params=pltpu.CompilerParams(vmem_limit_bytes=24 * 2**20),
    )(table, coup)


def pick_kernel(picks, table, *refs):
    nets, out = refs[:-1], refs[-1]
    depth = nets[0].shape[0]
    for q, net in enumerate(nets):
        for k, pick in enumerate(picks):
            at = pick(table, q)
            out[q * depth : (q + 1) * depth, k * BS : (k + 1) * BS] = kept(
                at >= 0, net[:, pl.ds(block_start(at), BS)]
            )


def pick_columns(picks, table, nets):
    return pl.pallas_call(
        lambda *refs: pick_kernel(picks, *refs),
        out_shape=jax.ShapeDtypeStruct(
            (len(nets) * nets[0].shape[0], len(picks) * BS), nets[0].dtype
        ),
        in_specs=[pl.BlockSpec(memory_space=pltpu.SMEM)]
        + [pl.BlockSpec(memory_space=pltpu.VMEM)] * len(nets),
        out_specs=pl.BlockSpec(memory_space=pltpu.VMEM),
        compiler_params=pltpu.CompilerParams(vmem_limit_bytes=24 * 2**20),
    )(table, *nets)


def front_kernel(lay, table, l_row, far_row, l_sep, far_sep, n_rows, n_sep, *refs):
    coups, (below, r_own, r_far) = refs[:-3], refs[-3:]
    group = table[lay.first] // 2 + pl.program_id(0)
    for p, row, out in ((0, l_row, r_own), (1, far_row, r_far)):
        for h in range(2):
            src = lay.upd_at(table, NODE + p, 2 * group + h)
            out[h * BS : (h + 1) * BS, :] = kept(src >= 0, row[pl.ds(pair_start(src), BS), :])
    value = jnp.dot(n_rows[...], n_sep[...], preferred_element_type=jnp.float32)
    for ref in coups:
        value = value + ref[...].astype(jnp.float32)
    value = value - outer(r_own[...], l_sep[...])
    below[...] = value - outer(r_far[...], far_sep[...])


def front(lay, table, l_row, far_row, l_sep, far_sep, n_rows, n_sep, coups):
    rows, sep = l_row.shape
    nets = n_rows.shape[1]
    strip = pl.BlockSpec((2 * BS, sep), lambda i: (i, 0))
    fixed = pl.BlockSpec((sep, sep), lambda i: (0, 0))
    picked = jax.ShapeDtypeStruct((rows, sep), l_row.dtype)
    return pl.pallas_call(
        lambda *refs: front_kernel(lay, *refs),
        grid=(rows // (2 * BS),),
        out_shape=(jax.ShapeDtypeStruct((rows, sep), jnp.float32), picked, picked),
        in_specs=[
            pl.BlockSpec(memory_space=pltpu.SMEM),
            strip,
            strip,
            fixed,
            fixed,
            pl.BlockSpec((2 * BS, nets), lambda i: (i, 0)),
            pl.BlockSpec((nets, sep), lambda i: (0, 0)),
        ]
        + [strip] * len(coups),
        out_specs=(strip, strip, strip),
        compiler_params=pltpu.CompilerParams(vmem_limit_bytes=24 * 2**20),
    )(table, l_row, far_row, l_sep, far_sep, n_rows, n_sep, *coups)


def copy_kernel(table, rows, out):
    out[...] = rows[...]


def pick_rows(lay, table, row, rows):
    width = rows.shape[1]
    spec = pltpu.PrefetchScalarGridSpec(
        num_scalar_prefetch=1,
        grid=(lay.sep,),
        in_specs=[
            pl.BlockSpec((BS, width), lambda i, t: (jnp.maximum(t[row * lay.per + i], 0), 0))
        ],
        out_specs=pl.BlockSpec((BS, width), lambda i, t: (i, 0)),
    )
    return pl.pallas_call(
        copy_kernel,
        out_shape=jax.ShapeDtypeStruct((lay.sep * BS, width), rows.dtype),
        grid_spec=spec,
    )(table, rows)


def merge_kernel(
    lay, table, own, *refs
):
    bulk = refs[:15]
    (l_own, l_far, l_new, n_all, r_own, r_far, r_new, n_rows, out) = refs[15:24]
    left, right, turn, turned = refs[24:]
    rows, tile = out.shape
    sep = l_own.shape[1]
    step = pl.program_id(0)
    kind, side = step // 2, step % 2
    first_row = table[lay.first]
    col_tile = (table[lay.first + 1 + kind] * 2 + side) * (tile // BS)
    even = table[lay.first] // (rows // BS) % 2 == 0
    others = (1, 2, 3)

    @pl.when(step == 0)
    def _():
        left[:, :sep] = -r_own[...]
        left[:, sep : 2 * sep] = -r_far[...]
        left[:, 2 * sep : 3 * sep] = -r_new[...]
        left[:, 3 * sep :] = n_rows[...]
        lane = lax.broadcasted_iota(jnp.int32, (BS, 2 * BS), 1)
        row = lax.broadcasted_iota(jnp.int32, (BS, 2 * BS), 0)
        for r in range(rows // BS):
            for n, q in enumerate(others):
                at = lay.upd_at(table, BOTH + q, first_row + r)
                hit = (lane == row + pair_start(at)) & (at >= 0)
                turn[r * BS : (r + 1) * BS, n * PIECE : (n + 1) * PIECE] = jnp.where(
                    hit, 1.0, 0.0
                ).astype(jnp.bfloat16)

    def col_of(piece, c):
        return col_tile + piece * 2 + c

    def add(ref, q, r, piece, c, value):
        row_at = lay.upd_at(table, BOTH + q, first_row + r)
        col_at = lay.upd_at(table, BOTH + q, col_of(piece, c))
        row_off = pl.multiple_of(pair_start(row_at) + (r // 2) * 2 * BS, BS)
        col_off = pl.multiple_of(pair_start(col_at) + piece * PIECE, BS)
        got = ref[pl.ds(row_off, BS), pl.ds(col_off, BS)].astype(jnp.float32)
        return value + jnp.where((row_at >= 0) & (col_at >= 0), got, 0.0)

    for piece in range(tile // PIECE):
        for p, ref in ((0, l_own), (1, l_far)):
            for c in range(2):
                at = lay.upd_at(table, NODE + p, col_of(piece, c))
                off = pl.multiple_of(pair_start(at) + piece * PIECE, BS)
                right[c * BS : (c + 1) * BS, p * sep : (p + 1) * sep] = kept(
                    at >= 0, ref[pl.ds(off, BS), :]
                )
        cols = slice(piece * PIECE, (piece + 1) * PIECE)
        right[:, 2 * sep : 3 * sep] = l_new[cols, :]
        right[:, 3 * sep :] = n_all[cols, :]
        for r in range(0, rows // BS, 2):
            prod = outer(left[r * BS : (r + 2) * BS, :], right[...])
            for h in range(2):
                for c in range(2):
                    value = prod[h * BS : (h + 1) * BS, c * BS : (c + 1) * BS]
                    at = piece * PIECE + c * BS
                    out[(r + h) * BS : (r + h + 1) * BS, at : at + BS] = add(
                        own, 0, r + h, piece, c, value
                    )

    def direct(sources):
        for piece in range(tile // PIECE):
            for r in range(rows // BS):
                for c in range(2):
                    spot = (
                        slice(r * BS, (r + 1) * BS),
                        slice(piece * PIECE + c * BS, piece * PIECE + (c + 1) * BS),
                    )
                    value = out[spot]
                    for q, ref in zip(others, sources):
                        value = add(ref, q, r, piece, c, value)
                    out[spot] = value

    def transposed(sources):
        width = len(others) * PIECE
        for piece in range(tile // PIECE):
            for c in range(2):
                for n, (q, ref) in enumerate(zip(others, sources)):
                    at = lay.upd_at(table, BOTH + q, col_of(piece, c))
                    off = pl.multiple_of(pair_start(at) + piece * PIECE, BS)
                    got = kept(at >= 0, ref[pl.ds(off, BS), :])
                    for g in range(rows // PIECE):
                        to = g * width + n * PIECE
                        turned[c * BS : (c + 1) * BS, to : to + PIECE] = got[
                            :, g * PIECE : (g + 1) * PIECE
                        ]
            cols = slice(piece * PIECE, (piece + 1) * PIECE)
            for g in range(rows // PIECE):
                spot = slice(g * PIECE, (g + 1) * PIECE)
                out[spot, cols] = out[spot, cols] + outer(
                    turn[spot, :], turned[:, g * width : (g + 1) * width]
                )

    for case, run, at in (
        (kind == 0, direct, 0),
        (kind == 1, direct, 3),
        (kind == 2, transposed, 6),
        ((kind == 3) & even, direct, 9),
        ((kind == 3) & jnp.logical_not(even), transposed, 12),
    ):

        @pl.when(case)
        def _(run=run, at=at):
            run(bulk[at : at + 3])


def merge(lay, table, own, diag, follow, turned, extra, extra_turned, factors, n_all, rows_of, n_rows):
    rows, cols = own.shape
    sep = factors[0].shape[1]
    nets = n_all.shape[1]
    depth = 3 * sep + nets
    strip_at = lambda i, t: t[lay.first + 1 + i // 2] * 2 + i % 2
    once = pl.Buffered(1)
    whole = lambda width: pl.BlockSpec((rows, width), lambda i, t: (0, 0), pipeline_mode=once)
    strip = lambda width: pl.BlockSpec((TILE, width), lambda i, t: (strip_at(i, t), 0))
    tile = pl.BlockSpec((rows, TILE), lambda i, t: (0, strip_at(i, t)))

    def wide(k):
        return pl.BlockSpec((rows, TILE), lambda i, t: (0, jnp.clip(i - 2 * k, 0, 1)))

    def tall(k):
        return pl.BlockSpec((TILE, rows), lambda i, t: (jnp.clip(i - 2 * k, 0, 1), 0))

    spec = pltpu.PrefetchScalarGridSpec(
        num_scalar_prefetch=1,
        grid=(cols // TILE,),
        in_specs=[tile]
        + [wide(0)] * 3
        + [wide(1)] * 3
        + [tall(2)] * 3
        + [wide(3)] * 3
        + [tall(3)] * 3
        + [strip(sep)] * 3
        + [strip(nets)]
        + [whole(sep)] * 3
        + [whole(nets)],
        out_specs=tile,
        scratch_shapes=[
            pltpu.VMEM((rows, depth), jnp.bfloat16),
            pltpu.VMEM((PIECE, depth), jnp.bfloat16),
            pltpu.VMEM((rows, 3 * PIECE), jnp.bfloat16),
            pltpu.VMEM((PIECE, 3 * rows), jnp.bfloat16),
        ],
    )
    return pl.pallas_call(
        lambda *refs: merge_kernel(lay, *refs),
        out_shape=jax.ShapeDtypeStruct((rows, cols), jnp.float32),
        grid_spec=spec,
        compiler_params=pltpu.CompilerParams(vmem_limit_bytes=56 * 2**20),
        cost_estimate=pl.CostEstimate(
            flops=2 * rows * cols * depth,
            bytes_accessed=12 * rows * cols + 2 * cols * depth,
            transcendentals=0,
        ),
    )(
        table, own, *diag, *follow, *turned, *extra, *extra_turned, *factors, n_all, *rows_of, n_rows
    )


def plain_merge_kernel(
    table, own, oth, far, low, high, l_own, l_far, l_new, n_all,
    r_own, r_far, r_new, n_rows, out, left, right,
):
    rows, tile = out.shape
    sep = l_own.shape[1]
    step = pl.program_id(0)
    half = pl.num_programs(0) // 2
    per = (table.shape[0] - 1) // 6
    first_row = table[6 * per]

    @pl.when(step == 0)
    def _():
        left[:, :sep] = -r_own[...]
        left[:, sep : 2 * sep] = -r_far[...]
        left[:, 2 * sep : 3 * sep] = -r_new[...]
        left[:, 3 * sep :] = n_rows[...]

    def spot(kind, block):
        at = table[kind * per + block]
        return at, pl.multiple_of((jnp.maximum(at, 0) % 2) * BS, BS)

    def add(ref, kind, r, piece, c, value):
        row_at, row_off = spot(kind, first_row + r)
        col_at, col_off = spot(kind, step * (tile // BS) + piece * 2 + c)
        row_off = pl.multiple_of(row_off + (r // 2) * 2 * BS, BS)
        col_off = pl.multiple_of(col_off + piece * PIECE, BS)
        got = ref[pl.ds(row_off, BS), pl.ds(col_off, BS)].astype(jnp.float32)
        return value + jnp.where((row_at >= 0) & (col_at >= 0), got, 0.0)

    for piece in range(tile // PIECE):
        for kind, ref in ((4, l_own), (5, l_far)):
            for c in range(2):
                at, off = spot(kind, step * (tile // BS) + piece * 2 + c)
                off = pl.multiple_of(off + piece * PIECE, BS)
                got = ref[pl.ds(off, BS), :]
                right[c * BS : (c + 1) * BS, (kind - 4) * sep : (kind - 3) * sep] = jnp.where(
                    at >= 0, got, jnp.zeros_like(got)
                )
        cols = slice(piece * PIECE, (piece + 1) * PIECE)
        right[:, 2 * sep : 3 * sep] = l_new[cols, :]
        right[:, 3 * sep :] = n_all[cols, :]
        for r in range(0, rows // BS, 2):
            prod = outer(left[r * BS : (r + 2) * BS, :], right[...])
            for h in range(2):
                for c in range(2):
                    value = prod[h * BS : (h + 1) * BS, c * BS : (c + 1) * BS]
                    for kind, ref in ((0, own), (1, oth), (2, far)):
                        value = add(ref, kind, r + h, piece, c, value)
                    at = piece * PIECE + c * BS
                    out[(r + h) * BS : (r + h + 1) * BS, at : at + BS] = value

    for side, ref in ((step < half, low), (step >= half, high)):

        @pl.when(side)
        def _(ref=ref):
            for piece in range(tile // PIECE):
                for r in range(rows // BS):
                    for c in range(2):
                        at = piece * PIECE + c * BS
                        spot_rows = slice(r * BS, (r + 1) * BS)
                        out[spot_rows, at : at + BS] = add(
                            ref, 3, r, piece, c, out[spot_rows, at : at + BS]
                        )


def plain_merge(block_first, comp, node_upd, coups, factors, n_all, rows_of, n_rows):
    own, oth, far, low, high = coups
    rows, cols = own.shape
    sep = factors[0].shape[1]
    nets = n_all.shape[1]
    steps = cols // TILE
    half = steps // 2
    table = jnp.concatenate(
        [comp.reshape(-1), node_upd.reshape(-1), jnp.int32(block_first)[None]]
    )
    depth = 3 * sep + nets
    whole = lambda width: pl.BlockSpec((rows, width), lambda i: (0, 0))
    strip = lambda width: pl.BlockSpec((TILE, width), lambda i: (i, 0))
    tile = pl.BlockSpec((rows, TILE), lambda i: (0, i))
    return pl.pallas_call(
        plain_merge_kernel,
        grid=(steps,),
        out_shape=jax.ShapeDtypeStruct((rows, cols), jnp.float32),
        in_specs=[
            pl.BlockSpec(memory_space=pltpu.SMEM),
            tile,
            tile,
            tile,
            pl.BlockSpec((rows, TILE), lambda i: (0, jnp.minimum(i, half - 1))),
            pl.BlockSpec((rows, TILE), lambda i: (0, jnp.maximum(i - half, 0))),
            strip(sep),
            strip(sep),
            strip(sep),
            strip(nets),
            whole(sep),
            whole(sep),
            whole(sep),
            whole(nets),
        ],
        out_specs=pl.BlockSpec((rows, TILE), lambda i: (0, i)),
        scratch_shapes=[
            pltpu.VMEM((rows, depth), jnp.bfloat16),
            pltpu.VMEM((PIECE, depth), jnp.bfloat16),
        ],
        compiler_params=pltpu.CompilerParams(vmem_limit_bytes=52 * 2**20),
        cost_estimate=pl.CostEstimate(
            flops=2 * rows * cols * depth,
            bytes_accessed=12 * rows * cols + 2 * cols * depth,
            transcendentals=0,
        ),
    )(table, own, oth, far, low, high, *factors, n_all, *rows_of, n_rows)


def leaf_spread(value, source_of, step):
    leaf_count, blk_count = lax.axis_size("leaf"), lax.axis_size("blk")
    sources = jnp.array([source_of(b) for b in range(blk_count)], jnp.int32)
    rank = lax.axis_index("leaf") ^ sources[lax.axis_index("blk")]
    pairs = []
    for b in range(blk_count):
        for r in range(0, leaf_count, 2 * step):
            src = source_of(b)
            pairs.append(((r ^ src) * blk_count + b, ((r + step) ^ src) * blk_count + b))
    got = lax.ppermute(value, ("leaf", "blk"), pairs)
    return jnp.where(rank % (2 * step) == step, got, value)


def first_two_far(value):
    blk_count = lax.axis_size("blk")
    blk_pos = lax.axis_index("blk")
    step = 2
    while step < blk_count:
        got = lax.ppermute(value, "blk", [(s, s + step) for s in range(step)])
        value = jnp.where((blk_pos >= step) & (blk_pos < 2 * step), got, value)
        step *= 2
    return value


def first_two_near(value):
    mate = swapped(value, "blk", 1)
    even = lax.axis_index("blk") % 2 == 0
    return jnp.where(even, value, mate), jnp.where(even, mate, value)


class Link:
    def __init__(self):
        self.last = None

    def __call__(self, send, value):
        if self.last is not None:
            value, _ = lax.optimization_barrier((value, self.last))
        self.last = send(value)
        return self.last


def per_device(leaf_net, leaf_coupling, index_maps, sep_anchor, top_net, top_coupling):
    leaf_count, blk_count = lax.axis_size("leaf"), lax.axis_size("blk")
    leaf_pos, blk_pos = lax.axis_index("leaf"), lax.axis_index("blk")
    net_own = leaf_net[0]
    coup_own = leaf_coupling[0]
    rows_dev, upd_order = coup_own.shape
    sep_order = sep_anchor.shape[1]
    block_rows = rows_dev // BS
    lay = Layout(sep_order // BS, upd_order // BS)
    block_first = blk_pos * block_rows
    node = leaf_pos >> 1
    triangle = blk_count == 4
    f32 = lambda value: value.astype(jnp.float32)
    tie = lax.optimization_barrier

    def among(options):
        return jnp.array(options, jnp.int32)[blk_pos]

    follow_to = (2, 3, 1, 0)
    places = [block_first]
    if triangle:
        places += [blk_pos, among(follow_to), among((3, 2, 0, 1)), blk_pos ^ 1]
    who = [leaf_pos ^ q for q in range(4)] + [leaf_count + node, leaf_count + (node ^ 1)]
    table = make_table(index_maps, lay.sep, jnp.stack(who + places))

    lead = 2 * PW
    rows_top = top_net.shape[1]
    same_source = blk_count * PW <= rows_top

    def spread(values, step):
        if same_source:
            return (leaf_spread(values[0], lambda b: 0, step),)
        return (
            leaf_spread(values[0], lambda b: 0, step),
            leaf_spread(values[1], lambda b: (b * PW) // rows_top, step),
        )

    piece = lax.dynamic_slice_in_dim(top_net, (blk_pos * PW) % rows_top, PW, 1)
    ours = (top_coupling[:lead], piece)
    if same_source:
        ours = (jnp.concatenate(ours, axis=0),)

    def leaf_even(mask):
        pairs = [
            (l * blk_count + b, (l ^ mask) * blk_count + b)
            for l in range(leaf_count)
            for b in range(0, blk_count, 2)
        ]
        return lambda value: lax.ppermute(value, ("leaf", "blk"), pairs)

    def turn(value):
        return lax.ppermute(value, "blk", [(b, follow_to[b]) for b in range(blk_count)])

    def to_odd(value):
        return lax.ppermute(value, "blk", [(b, b + 1) for b in range(0, blk_count, 2)])

    def block(src, c):
        return lax.dynamic_slice_in_dim(src, c * rows_dev, rows_dev, 1)

    across_y, across_z, across_x = Link(), Link(), Link()
    near = lambda value: across_y(lambda v: swapped(v, "leaf", 1), value)
    far = lambda value: across_z(lambda v: swapped(v, "leaf", 2), value)

    net_oth = near(net_own)
    c1_own, s1, c2_own, s2 = extract(lay, table, coup_own)
    s1_own = across_x(lambda v: total(v, "blk"), s1)
    s1_oth = near(s1_own)
    ours, _ = tie((ours, table))
    step = leaf_count // 2
    while step >= 4:
        ours = across_z(lambda v: spread(v, step), ours)
        step //= 2
    c2_far = far(c2_own)
    ours = across_z(lambda v: spread(v, 2), ours)
    net_far = far(jnp.concatenate([net_own, net_oth], axis=1))
    net_far, net_far_oth = net_far[:, :upd_order], net_far[:, upd_order:]
    s2_own = across_x(lambda v: total(v, "blk"), s2)
    c1_oth, s2_oth = near(c1_own), near(s2_own)
    c2_oth, c2_far_oth = near(c2_own), near(c2_far)
    ours = across_y(lambda v: spread(v, 1), ours)
    s2_far = far(jnp.concatenate([s2_own, s2_oth], axis=1))
    s2_far, s2_far_oth = s2_far[:, :sep_order], s2_far[:, sep_order:]

    pick1 = [lambda t, q, s=s: lay.sep_at(t, LEAF + q, s) for s in range(lay.sep)]
    pick1 += [
        lambda t, q, i=i: lay.upd_at(t, LEAF + q, t[lay.first] + i) for i in range(block_rows)
    ]
    n1 = pick_columns(pick1, table, [net_own, net_oth])
    n1_sep, n1_rows = n1[:, :sep_order], n1[:, sep_order:]
    pivot = gram(n1_sep, n1_sep) + f32(s1_own) + f32(s1_oth) + jnp.diag(sep_anchor[node])
    low1 = inverse_factor(pivot)
    below = gram(n1_rows, n1_sep) + f32(c1_own) + f32(c1_oth)
    lrow1 = solved(below, low1).astype(jnp.bfloat16)
    l_own = lax.all_gather(lrow1, "blk", axis=0, tiled=True)
    lrow1_far = swapped(lrow1, "leaf", 2)
    l_sep = pick_rows(lay, table, NODE, l_own)
    l_sep_far = swapped(l_sep, "leaf", 2)

    if same_source:
        lead_mine, net_mine = ours[0][:lead], ours[0][lead:]
        both0, both1 = first_two_near(across_x(first_two_far, ours[0]))
    else:
        lead_mine, net_mine = ours
        both0, both1 = first_two_near(
            across_x(first_two_far, jnp.concatenate(ours, axis=0))
        )
    coup_even_odd = across_x(first_two_far, top_coupling)
    l_far = lax.all_gather(lrow1_far, "blk", axis=0, tiled=True)

    if triangle:
        follow0 = block(coup_own, among(follow_to))
        diag0, extra0 = block(coup_own, blk_pos), block(coup_own, blk_pos ^ 1)
        follow_z, _ = tie((follow0, l_sep_far))
        follow1, follow2 = near(follow0), far(follow_z)

    pick2 = [lambda t, q, s=s: lay.sep_at(t, BOTH + q, s) for s in range(lay.sep)]
    pick2 += [lambda t, q, m=m: lay.upd_at(t, BOTH + q, m) for m in range(upd_order // BS)]
    n2 = pick_columns(pick2, table, [net_own, net_oth, net_far, net_far_oth])
    n2_sep = n2[:, :sep_order]
    n_all = n2[:, sep_order:].T
    n_rows = lax.dynamic_slice_in_dim(n_all, blk_pos * rows_dev, rows_dev, 0)

    below, r_own, r_far = front(
        lay, table, lrow1, lrow1_far, l_sep, l_sep_far, n_rows, n2_sep,
        (c2_own, c2_oth, c2_far, c2_far_oth),
    )
    pivot = gram(n2_sep, n2_sep) + f32(s2_own) + f32(s2_oth) + f32(s2_far) + f32(s2_far_oth)
    pivot = pivot - outer(l_sep, l_sep) - outer(l_sep_far, l_sep_far)
    low2 = inverse_factor(pivot + jnp.diag(sep_anchor[leaf_count // 2 + (node >> 1)]))
    r_new = solved(below, low2).astype(jnp.bfloat16)
    l_new = lax.all_gather(r_new, "blk", axis=0, tiled=True)

    if triangle:
        r_new, follow1, follow2, both0, both1 = tie((r_new, follow1, follow2, both0, both1))
        diag1, follow3 = near(diag0), far(follow1)
        turned1 = across_x(turn, follow1)
        extra1, diag2 = across_y(leaf_even(1), extra0), far(diag0)
        turned2 = across_x(turn, follow2)
        extra2 = across_z(leaf_even(2), extra0)
        diag3 = near(diag2)
        turned3 = across_x(turn, follow3)
        extra3 = across_y(leaf_even(1), extra2)
        low_extra1, low_extra2, low_extra3 = to_odd(extra1), to_odd(extra2), to_odd(extra3)

    coup0, coup1 = first_two_near(coup_even_odd)
    lead0, net0 = f32(both0[:lead]), both0[lead:]
    lead1, net1 = f32(both1[:lead]), both1[lead:]
    mine = f32(lead_mine)
    inv0 = inverse_factor(gram(net0, net0) + lead0[:PW])
    cross = solved(gram(net1, net0) + lead0[PW:], inv0).astype(jnp.bfloat16)
    inv1 = inverse_factor(gram(net1, net1) + lead1[PW:] - outer(cross, cross))

    row = (leaf_pos * rows_top + jnp.arange(rows_top, dtype=jnp.int32))[:, None]
    col = jnp.arange(PW, dtype=jnp.int32)[None, :]

    def panel(current, low, first):
        return jnp.where(row - first >= col, solved(current, low), 0.0)

    q0 = solved((gram(net0, net_mine) + mine[:PW]).T, inv0).astype(jnp.bfloat16)
    q1 = solved((gram(net1, net_mine) + mine[PW:]).T - outer(q0, cross), inv1)
    q1 = q1.astype(jnp.bfloat16)
    p0 = panel(gram(top_net, net0) + f32(coup0), inv0, 0)
    b0 = p0.astype(jnp.bfloat16)
    x1 = gram(top_net, net1) + f32(coup1) - outer(b0, cross)
    p1 = panel(x1, inv1, PW)
    rest = gram(top_net, net_mine) + f32(top_coupling) - outer(b0, q0)
    rest = rest - outer(p1.astype(jnp.bfloat16), q1)
    window = jnp.where(blk_pos == 0, p0, jnp.where(blk_pos == 1, p1, rest))

    factors, rows_of = (l_own, l_far, l_new), (r_own, r_far, r_new)
    if triangle:
        update = merge(
            lay, table, coup_own,
            (diag1, diag2, diag3),
            (follow1, follow2, follow3),
            (turned1, turned2, turned3),
            (extra1, extra2, extra3),
            (low_extra1, low_extra2, low_extra3),
            factors, n_all, rows_of, n_rows,
        )
    else:
        half = upd_order // 2
        bulk_oth, bulk_far = swapped(coup_own, "leaf", 1), swapped(coup_own, "leaf", 2)
        bulk_low = swapped(bulk_oth[:, :half], "leaf", 2)
        bulk_high = swapped(bulk_far[:, half:], "leaf", 1)
        split = table[: lay.first].reshape(10, lay.per)
        update = plain_merge(
            block_first, split[BOTH:, lay.sep :], split[NODE:BOTH, lay.sep :],
            (coup_own, bulk_oth, bulk_far, bulk_low, bulk_high),
            factors, n_all, rows_of, n_rows,
        )
    return (update[None], window)


def solution(mesh):
    return jax.shard_map(
        per_device,
        mesh=mesh,
        in_specs=(
            P("leaf", None, None),
            P("leaf", "blk", None),
            P(),
            P(),
            P(None, "leaf"),
            P("leaf", "blk"),
        ),
        out_specs=(P("leaf", "blk", None), P("leaf", "blk")),
        check_vma=False,
    )
```
